32 devices in a mesh: kx: 8 (over z, y), ky: 4 (over x, core).
Axes of the slice: x: 2, y: 2, z: 4, core: 2. Of those that a mesh axis runs over, the one named last changes fastest.
Arguments:
- vectors: bfloat16 [2, 8, 8, 2, 16, 1024], P(None, 'kx', 'ky'), may hold values from -1.1953125 to 1.1953125
- density: bfloat16 [2, 8, 8, 2, 16, 16], P(None, 'kx', 'ky'), may hold values from -1 to 1
- coulomb: float32 [4, 7], replicated, may hold values from 0.3 to 3
- shells: int32 [4, 7, 2], replicated, may hold values from -1 to 1
- shift_x: int32 [4], replicated, may hold values from 0 to 7
- shift_y: int32 [4], replicated, may hold values from 0 to 7
Outputs:
- exchange: float32 [2, 8, 8, 2, 16, 16], P(None, 'kx', 'ky')
The draws below stay inside these ranges and needn't reach their ends.
All inputs are finite; a program needn't handle non-finite values.
Results may differ from the reference program's by a relative error of at most 0.0004.
Values may be sent and summed in bfloat16 or wider, within the bound.
No kernel may reach another device: no remote copies, remote signals or barrier semaphores. Data moves between devices by JAX's collectives and lax.ppermute only.
A program may use at most 64 MiB of HBM per device.

```python
import math
import jax
import jax.numpy as jnp
from jax import lax

FL = 2
NB = 16
GA = 16
GB = 16
NPW = 1024
NKX = 8
NKY = 8
Q = 4
NSH = 7


def with_ends(values, rng, smallest, high):
    shape = values.shape
    index_at = [jax.random.randint(jax.random.fold_in(rng, axis), (), 0, shape[axis]) for axis in range(len(shape))]
    values = values.at[tuple(index_at)].set(smallest)
    longest = shape.index(max(shape))
    index_at[longest] = (index_at[longest] + 1) % shape[longest]
    return values.at[tuple(index_at)].set(high)


def level_of(stream_key, extent, pieces, smallest, top_value):
    factor_of = 1.0
    for dim, shards_of in pieces:
        heights = jax.random.uniform(jax.random.fold_in(jax.random.fold_in(stream_key, 6), dim), (shards_of,), jnp.float32, smallest / len(pieces), top_value / len(pieces))
        factor_of = factor_of * jnp.repeat(jnp.exp(heights), extent[dim] // shards_of).reshape((-1,) + (1,) * (len(extent) - 1 - dim))
    return factor_of


def centred(key, extent, width, bound, cuts=(), dtype=jnp.bfloat16):
    drawn = width * jax.random.normal(key, extent, jnp.float32)
    if cuts:
        drawn = drawn * level_of(key, extent, cuts, -0.22, 0.18)
    return jnp.clip(drawn, -bound, bound).astype(dtype)


def setup_inputs(seed: int = 0) -> dict:
    arg_keys = jax.random.split(jax.random.key(seed), 7)
    return {
        "vectors": centred(arg_keys[0], (2, NKX, NKY, FL, NB, NPW), 0.1768, 1.1953125, ((1, 8), (2, 4))),
        "density": centred(arg_keys[1], (2, NKX, NKY, FL, NB, NB), 0.15, 1.0, ((1, 8), (2, 4))),
        "coulomb": jnp.clip(jnp.exp(jax.random.uniform(arg_keys[2], (Q, NSH), jnp.float32, math.log(0.3), math.log(3.0))), 0.3, 3.0),
        "shells": with_ends(jax.random.randint(arg_keys[3], (Q, NSH, 2), -1, 2), jax.random.fold_in(arg_keys[3], 1), -1, 1).astype(jnp.int32),
        "shift_x": with_ends(jax.random.randint(arg_keys[4], (Q,), 0, NKX), jax.random.fold_in(arg_keys[4], 1), 0, NKX - 1).astype(jnp.int32),
        "shift_y": with_ends(jax.random.randint(arg_keys[5], (Q,), 0, NKY), jax.random.fold_in(arg_keys[5], 1), 0, NKY - 1).astype(jnp.int32),
    }


highest = lax.Precision.HIGHEST
shift_pairs = [(row_shift, col_shift) for row_shift in (-1, 0, 1, 2) for col_shift in (-1, 0, 1, 2)]


def shifted_planes(planes, row_shift, col_shift):
    length = planes.shape[-1]
    margin = 2 * GB + 2
    padded = jnp.pad(planes, [(0, 0)] * (planes.ndim - 1) + [(margin, margin)])
    offset = row_shift * GB + col_shift
    window = padded[..., margin + offset:margin + offset + length]
    position = jnp.arange(length) % (GA * GB)
    row_index = position // GB + row_shift
    col_index = position % GB + col_shift
    inside = (row_index >= 0) & (row_index < GA) & (col_index >= 0) & (col_index < GB)
    return jnp.where(inside, window, jnp.zeros_like(window))


def form_factors(local_vectors, arrived):
    stacked = jnp.stack([shifted_planes(arrived, row_shift, col_shift) for row_shift, col_shift in shift_pairs])
    blocks = jnp.einsum("rpfmg,stpfng->srtpfmn", local_vectors, stacked, preferred_element_type=jnp.float32, precision=highest)
    lam_re = blocks[:, 0, 0] + blocks[:, 1, 1]
    lam_im = blocks[:, 0, 1] - blocks[:, 1, 0]
    return lam_re, lam_im


def exchange_terms(lam_re, lam_im, den_re, den_im):
    left_re = jnp.einsum("spfmn,pfnk->spfmk", lam_re, den_re, precision=highest) - jnp.einsum("spfmn,pfnk->spfmk", lam_im, den_im, precision=highest)
    left_im = jnp.einsum("spfmn,pfnk->spfmk", lam_re, den_im, precision=highest) + jnp.einsum("spfmn,pfnk->spfmk", lam_im, den_re, precision=highest)
    term_re = jnp.einsum("spfmk,spfjk->spfmj", left_re, lam_re, precision=highest) + jnp.einsum("spfmk,spfjk->spfmj", left_im, lam_im, precision=highest)
    term_im = jnp.einsum("spfmk,spfjk->spfmj", left_im, lam_re, precision=highest) - jnp.einsum("spfmk,spfjk->spfmj", left_re, lam_im, precision=highest)
    return term_re, term_im


def shell_weights(coulomb_row, shell_row, wrap_x, wrap_y):
    pair_rows = jnp.array([pair[0] for pair in shift_pairs], jnp.int32)
    pair_cols = jnp.array([pair[1] for pair in shift_pairs], jnp.int32)
    match_x = (shell_row[None, :, 0] + wrap_x) == pair_rows[:, None]
    match_y = (shell_row[None, :, 1, None] + wrap_y[None, None, :]) == pair_cols[:, None, None]
    chosen = jnp.where(match_x[:, :, None] & match_y, coulomb_row[None, :, None], jnp.zeros_like(coulomb_row)[None, :, None])
    return jnp.sum(chosen, axis=1)


def reference(vectors, density, coulomb, shells, shift_x, shift_y):
    vec_all = vectors.astype(jnp.float32)
    den_all = density.astype(jnp.float32)
    ky_index = jnp.arange(NKY).astype(jnp.int32)
    accumulated = jnp.zeros((NKX, 2, NKY, FL, NB, NB), jnp.float32)
    for transfer in range(Q):
        step_x = shift_x[transfer]
        step_y = shift_y[transfer]
        arrived_vec = jnp.roll(vec_all, (-step_x, -step_y), axis=(1, 2))
        arrived_den = jnp.roll(den_all, (-step_x, -step_y), axis=(1, 2))
        wrap_y = (ky_index + step_y >= NKY).astype(jnp.int32)

        def row_terms(kx_row):
            local_vectors = lax.dynamic_index_in_dim(vec_all, kx_row, 1, keepdims=False)
            arrived = lax.dynamic_index_in_dim(arrived_vec, kx_row, 1, keepdims=False)
            arrived_p = lax.dynamic_index_in_dim(arrived_den, kx_row, 1, keepdims=False)
            wrap_x = (kx_row + step_x >= NKX).astype(jnp.int32)
            lam_re, lam_im = form_factors(local_vectors, arrived)
            term_re, term_im = exchange_terms(lam_re, lam_im, arrived_p[0], arrived_p[1])
            weights = shell_weights(coulomb[transfer], shells[transfer], wrap_x, wrap_y)
            part_re = jnp.einsum("sp,spfmn->pfmn", weights, term_re, precision=highest)
            part_im = jnp.einsum("sp,spfmn->pfmn", weights, term_im, precision=highest)
            return jnp.stack([part_re, part_im])

        accumulated = accumulated + lax.map(row_terms, jnp.arange(NKX).astype(jnp.int32))
    scale = -1.0 / (Q * NSH)
    return jnp.transpose(accumulated * scale, (1, 0, 2, 3, 4, 5))
```

```python
import jax
import jax.numpy as jnp
from jax import lax
from jax.experimental import pallas as pl
from jax.experimental.pallas import tpu as pltpu
from jax.sharding import PartitionSpec as P

GA = 16
GB = 16
LANES = 128
SPAN = 4
DIRECT = 8
HIGHEST = lax.Precision.HIGHEST


def ky_blocks(part, count):
    blocks = {0: part}
    bit = count // 2
    while bit:
        perm = [(i, i ^ bit) for i in range(count)]
        for off in list(blocks):
            blocks[off ^ bit] = lax.ppermute(blocks[off], "ky", perm)
        bit //= 2
    return [blocks[off] for off in range(count)]


def shift_bank_kernel(vec_ref, bank_ref):
    ri, _, per, fl, nb, npw = vec_ref.shape
    position = lax.broadcasted_iota(jnp.int32, (1, npw), 1)
    row = (position // GB) % GA
    col = position % GB
    masks = []
    for combo in range(SPAN * SPAN):
        s1, s2 = combo // SPAN - 1, combo % SPAN - 1
        inside = (row >= s1) & (row < GA + s1) & (col >= s2) & (col < GB + s2)
        masks.append(inside.astype(jnp.float32))

    def slab(i, carry):
        a, c, f = i // (per * fl), (i // fl) % per, i % fl
        x = vec_ref[a, 0, c, f].astype(jnp.float32)
        for combo in range(SPAN * SPAN):
            s1, s2 = combo // SPAN - 1, combo % SPAN - 1
            moved = pltpu.roll(x, (s1 * GB + s2) % npw, 1)
            bank_ref[combo, a, c, f] = (moved * masks[combo]).astype(jnp.bfloat16)
        return carry

    lax.fori_loop(0, ri * per * fl, slab, 0)


def shift_bank(vectors):
    ri, _, per, fl, nb, npw = vectors.shape
    return pl.pallas_call(
        shift_bank_kernel,
        out_shape=jax.ShapeDtypeStruct((SPAN * SPAN, ri, per, fl, nb, npw), jnp.bfloat16),
        name="shift_bank",
    )(vectors)


def select_kernel(pick_ref, *refs, count, per):
    vec_refs, den_refs, outs = refs[:count], refs[count : 2 * count], refs[2 * count :]
    ri, _, _, fl, nb, npw = vec_refs[0].shape
    tiles = npw // LANES
    rows = per * ri * fl * nb
    for j, out in enumerate(outs):
        for c in range(per):
            off = pick_ref[j, 2 * c]
            src = pick_ref[j, 2 * c + 1]
            for o in range(count):

                @pl.when(off == o)
                def _():
                    for a in range(ri):
                        for f in range(fl):
                            base = ((c * ri + a) * fl + f) * nb
                            x = vec_refs[o][a, 0, src, f]
                            for t in range(tiles):
                                out[pl.ds(t * rows + base, nb), :] = x[:, t * LANES : (t + 1) * LANES]
                    out[pl.ds(tiles * rows + c * nb, nb), :] = den_refs[o][src]


def select(pick, vec_blocks, den_blocks, per, transfers):
    ri, _, _, fl, nb, npw = vec_blocks[0].shape
    rows = per * ri * fl * nb * (npw // LANES) + per * nb
    count = len(vec_blocks)

    def kernel(*refs):
        select_kernel(*refs, count=count, per=per)

    vm = pl.BlockSpec(memory_space=pltpu.VMEM)
    return pl.pallas_call(
        kernel,
        in_specs=[pl.BlockSpec(memory_space=pltpu.SMEM)] + [vm] * (2 * count),
        out_specs=[vm] * transfers,
        out_shape=[jax.ShapeDtypeStruct((rows, LANES), jnp.bfloat16)] * transfers,
        name="select_columns",
    )(pick, *vec_blocks, *den_blocks)


def joint_pairs(mesh_shape, dx):
    kx, ky = mesh_shape
    return [(((x + dx) % kx) * ky + y, x * ky + y) for x in range(kx) for y in range(ky)]


def along_kx(parts, steps, kx_count, ky_count):
    def moved(part, dx):
        if dx % kx_count == 0:
            return part
        return lax.ppermute(part, ("kx", "ky"), joint_pairs((kx_count, ky_count), dx))

    place = 1
    while place < kx_count:
        left = kx_count // place
        radix = left if left <= DIRECT else 4
        digits = [(s // place) % radix for s in steps]

        def branch(a, b):
            return lambda x, y: (moved(x, a * place), moved(y, b * place))

        branches = [branch(a, b) for a in range(radix) for b in range(radix)]
        parts = lax.switch(digits[0] * radix + digits[1], branches, *parts)
        place *= radix
    return parts


def terms_kernel(combo_ref, weight_ref, bank_ref, *refs, nsh, scale):
    loads, out_ref = refs[:-1], refs[-1]
    _, ri, per, fl, nb, npw = bank_ref.shape
    tiles = npw // LANES
    rows = per * ri * fl * nb
    slots = LANES // nb
    lane = lax.broadcasted_iota(jnp.int32, (nb, LANES), 1)
    group = lane // nb

    def one(i, carry):
        c, f = i // fl, i % fl
        acc_re = jnp.zeros((nb, LANES), jnp.float32)
        acc_im = jnp.zeros((nb, LANES), jnp.float32)
        for j, load in enumerate(loads):
            arrived = [
                jnp.concatenate(
                    [
                        load[pl.ds(pl.multiple_of(t * rows + ((c * ri + b) * fl + f) * nb, nb), nb), :]
                        for t in range(tiles)
                    ],
                    axis=1,
                )
                for b in range(ri)
            ]
            arrived = jnp.concatenate(arrived, axis=0)
            shifted = jnp.concatenate(
                [bank_ref[combo_ref[j, c, min(l, nsh - 1)], a, c, f] for a in range(ri) for l in range(slots)],
                axis=0,
            )
            both = lax.dot_general(
                arrived, shifted, (((1,), (1,)), ((), ())), preferred_element_type=jnp.float32
            )
            lam_re = both[:nb, :LANES] + both[nb:, LANES:]
            lam_im = both[nb:, :LANES] - both[:nb, LANES:]
            lam = jnp.concatenate([lam_re, lam_im], axis=0)
            den = load[pl.ds(pl.multiple_of(tiles * rows + c * nb, nb), nb), :].astype(jnp.float32)
            den = jnp.where(f == 0, den, pltpu.roll(den, LANES - 2 * nb, 1))
            den_re, den_im = den[:, :nb], den[:, nb : 2 * nb]
            mix = jnp.concatenate(
                [
                    jnp.concatenate([den_re, -den_im], axis=1),
                    jnp.concatenate([den_im, den_re], axis=1),
                ],
                axis=0,
            )
            left = jnp.dot(mix, lam, precision=HIGHEST, preferred_element_type=jnp.float32)
            turned = jnp.concatenate([left[nb:], -left[:nb]], axis=0)
            both_left = jnp.concatenate([left, turned], axis=1).T
            gram = jnp.dot(both_left, lam, precision=HIGHEST, preferred_element_type=jnp.float32)
            for l in range(nsh):
                w = weight_ref[j, l]
                keep = group == l
                acc_re += jnp.where(keep, w * gram[l * nb : (l + 1) * nb], 0.0)
                acc_im += jnp.where(keep, w * gram[LANES + l * nb : LANES + (l + 1) * nb], 0.0)
        step = LANES // 2
        while step >= nb:
            acc_re += pltpu.roll(acc_re, step, 1)
            acc_im += pltpu.roll(acc_im, step, 1)
            step //= 2
        out_ref[0, 0, c, f] = acc_re[:, :nb] * scale
        out_ref[1, 0, c, f] = acc_im[:, :nb] * scale
        return carry

    lax.fori_loop(0, per * fl, one, 0)


def exchange_terms(combos, weights, bank, loads, scale):
    _, ri, per, fl, nb, npw = bank.shape

    def kernel(*refs):
        terms_kernel(*refs, nsh=weights.shape[1], scale=scale)

    sm = pl.BlockSpec(memory_space=pltpu.SMEM)
    vm = pl.BlockSpec(memory_space=pltpu.VMEM)
    return pl.pallas_call(
        kernel,
        in_specs=[sm, sm, vm] + [vm] * len(loads),
        out_specs=vm,
        out_shape=jax.ShapeDtypeStruct((ri, 1, per, fl, nb, nb), jnp.float32),
        name="exchange_terms",
    )(combos, weights, bank, *loads)


def body(vectors, density, coulomb, shells, shift_x, shift_y):
    kx_count, ky_count = lax.axis_size("kx"), lax.axis_size("ky")
    ri, _, per, fl, nb, npw = vectors.shape
    transfers, nsh = coulomb.shape
    span_y = per * ky_count
    me = lax.axis_index("ky")
    my_row = lax.axis_index("kx")
    cols = me * per + jnp.arange(per, dtype=jnp.int32)

    den = jnp.transpose(density[:, 0], (1, 4, 2, 0, 3)).reshape(per, nb, fl * ri * nb)
    den = jnp.pad(den, ((0, 0), (0, 0), (0, LANES - fl * ri * nb)))
    vec_blocks = ky_blocks(vectors, ky_count)
    den_blocks = ky_blocks(den, ky_count)
    wanted = (cols[None, :] + shift_y[:, None]) % span_y
    pick = jnp.stack([(wanted // per) ^ me, wanted % per], axis=2).reshape(transfers, 2 * per)
    loads = select(pick, vec_blocks, den_blocks, per, transfers)

    wrap_x = (my_row + shift_x >= kx_count).astype(jnp.int32)
    wrap_y = (cols[None, :] + shift_y[:, None] >= span_y).astype(jnp.int32)
    s1 = shells[:, None, :, 0] + wrap_x[:, None, None]
    s2 = shells[:, None, :, 1] + wrap_y[:, :, None]
    combos = (s1 + 1) * SPAN + (s2 + 1)
    bank = shift_bank(vectors)

    arrived = []
    for j in range(0, transfers, 2):
        arrived += along_kx(loads[j : j + 2], [shift_x[j], shift_x[j + 1]], kx_count, ky_count)
    return exchange_terms(combos, coulomb, bank, arrived, -1.0 / (transfers * nsh))


def solution(mesh):
    placed = (P(None, "kx", "ky"), P(None, "kx", "ky"), P(), P(), P(), P())
    return jax.shard_map(
        body, mesh=mesh, in_specs=placed, out_specs=P(None, "kx", "ky"), check_vma=False
    )
```

```python
import jax
import jax.numpy as jnp
from jax import lax
from jax.experimental import pallas as pl
from jax.experimental.pallas import tpu as pltpu
from jax.sharding import PartitionSpec as P

GA = 16
GB = 16
LANES = 128
SPAN = 4
PER_TILE = LANES // GB
PER_PLANE = GA // PER_TILE
DIRECT = 8
MIB = 1 << 20
VM = pl.BlockSpec(memory_space=pltpu.VMEM)
SM = pl.BlockSpec(memory_space=pltpu.SMEM)
ANY = pl.BlockSpec(memory_space=pl.ANY)


def params(mib):
    return pltpu.CompilerParams(vmem_limit_bytes=mib * MIB)


def pack_kernel(vec_ref, den_ref, out_ref):
    ri, _, per, fl, nb, npw = vec_ref.shape
    tiles = npw // LANES
    rows = ri * fl * nb
    for c in range(per):
        for a in range(ri):
            for f in range(fl):
                x = vec_ref[a, 0, c, f]
                for t in range(tiles):
                    out_ref[c, pl.ds(t * rows + (a * fl + f) * nb, nb), :] = x[:, t * LANES : (t + 1) * LANES]
        both = [den_ref[a, 0, c, f].astype(jnp.float32) for f in range(fl) for a in range(ri)]
        wide = jnp.concatenate(both * (LANES // (fl * ri * nb)), axis=1)
        out_ref[c, pl.ds(tiles * rows, nb), :] = wide.astype(jnp.bfloat16)


def pack(vectors, density):
    ri, _, per, fl, nb, npw = vectors.shape
    rows = ri * fl * nb * (npw // LANES) + nb
    return pl.pallas_call(
        pack_kernel,
        in_specs=[VM, VM],
        out_specs=VM,
        out_shape=jax.ShapeDtypeStruct((per, rows, LANES), jnp.bfloat16),
        compiler_params=params(4),
        name="pack_columns",
    )(vectors, density)


def start_columns(j, shift, me, blocks, dst, sem):
    count, per = len(blocks), blocks[0].shape[0]
    for c in range(per):
        wanted = (me * per + c + shift) % (per * count)
        off, src = (wanted // per) ^ me, wanted % per
        for o in range(count):

            @pl.when(off == o)
            def _():
                pltpu.make_async_copy(blocks[o].at[src], dst.at[c], sem.at[j, c]).start()


def wait_columns(j, blocks, dst, sem):
    for c in range(blocks[0].shape[0]):
        pltpu.make_async_copy(blocks[0].at[0], dst.at[c], sem.at[j, c]).wait()


def select(at, shift_y, blocks, which):
    def kernel(at_ref, shift_ref, *refs):
        ins, outs, sem = refs[: len(blocks)], refs[len(blocks) : -1], refs[-1]
        for i, j in enumerate(which):
            start_columns(i, shift_ref[j], at_ref[1], ins, outs[i], sem)
        for i, j in enumerate(which):
            wait_columns(i, ins, outs[i], sem)

    return pl.pallas_call(
        kernel,
        in_specs=[SM, SM] + [ANY] * len(blocks),
        out_specs=[ANY] * len(which),
        out_shape=[jax.ShapeDtypeStruct(blocks[0].shape, blocks[0].dtype)] * len(which),
        scratch_shapes=[pltpu.SemaphoreType.DMA((len(which), blocks[0].shape[0]))],
        compiler_params=params(1),
        name="select_columns",
    )(at, shift_y, *blocks)


def along_kx(parts, steps, kx_count, ky_count):
    def moved(part, dx):
        if dx % kx_count == 0:
            return part
        pairs = [
            (((x + dx) % kx_count) * ky_count + y, x * ky_count + y) for x in range(kx_count) for y in range(ky_count)
        ]
        return lax.ppermute(part, ("kx", "ky"), pairs)

    place = 1
    while place < kx_count:
        left = kx_count // place
        radix = left if left <= DIRECT else 4
        first, second = [s if radix == kx_count else (s // place) % radix for s in steps]

        def branch(a, b):
            return lambda x, y: (moved(x, a * place), moved(y, b * place))

        branches = [branch(a, b) for a in range(radix) for b in range(radix)]
        parts = lax.switch(first * radix + second, branches, *parts)
        place *= radix
    return parts


def across_ky(part, count, by):
    return lax.ppermute(part, "ky", [(i, i ^ by) for i in range(count)])


def column_shifts(vec_ref, cols_ref):
    ri, _, per, fl, nb, npw = vec_ref.shape
    col = lax.broadcasted_iota(jnp.int32, (nb, LANES), 1) % GB
    for a in range(ri):
        for c in range(per):
            for f in range(fl):
                for t in range(npw // LANES):
                    x = vec_ref[a, 0, c, f, :, t * LANES : (t + 1) * LANES]
                    for s2 in range(-1, SPAN - 1):
                        good = (col >= s2) & (col < GB + s2)
                        y = jnp.where(good, pltpu.roll(x, s2 % LANES, 1), jnp.zeros_like(x)) if s2 else x
                        cols_ref[s2 + 1, a, c, f, :, t * LANES : (t + 1) * LANES] = y


def row_shifted(tiles, s1, keep, above, below, zero):
    moved = [pltpu.roll(x, ((s1 + PER_TILE) % PER_TILE) * GB, 1) for x in tiles]
    out = []
    for t, x in enumerate(moved):
        other = zero
        if t % PER_PLANE > 0:
            other = jnp.where(above, moved[t - 1], other)
        if t % PER_PLANE < PER_PLANE - 1:
            other = jnp.where(below, moved[t + 1], other)
        out.append(jnp.where(keep, x, other))
    return out


def split(x):
    high = x.astype(jnp.bfloat16)
    return high, (x - high.astype(jnp.float32)).astype(jnp.bfloat16)


def nt(a, b):
    return lax.dot_general(a, b, (((1,), (1,)), ((), ())), preferred_element_type=jnp.float32)


def form_factors(cols_ref, moves, c, f, arrived, slots):
    _, ri, _, _, nb, npw = cols_ref.shape
    tiles = npw // LANES
    zero = jnp.zeros((nb, LANES), jnp.bfloat16)
    total = None
    for a in range(ri):
        own = []
        for s1, s2, keep, above, below in moves:
            slab = cols_ref[s2 + 1, a, c, f]
            pieces = [slab[:, t * LANES : (t + 1) * LANES] for t in range(tiles)]
            own.append(row_shifted(pieces, s1, keep, above, below, zero))
        own += [[zero] * tiles] * (slots - len(moves))
        for t in range(0, tiles, PER_PLANE):
            left = jnp.concatenate([jnp.concatenate(o[t : t + PER_PLANE], axis=1) for o in own], axis=0)
            at = a * npw + t * LANES
            part = nt(left, arrived[:, at : at + PER_PLANE * LANES])
            total = part if total is None else total + part
    return total


def transfer_sum(load, cols_ref, shift, weight, nsh):
    _, ri, per, fl, nb, npw = cols_ref.shape
    tiles = npw // LANES
    rows = ri * fl * nb
    lane = lax.broadcasted_iota(jnp.int32, (nb, LANES), 1)
    lane_row = lane // GB
    part_im = (lane // nb) % ri == 1
    unit = lane // (ri * nb)
    zero = jnp.zeros((nb, LANES), jnp.float32)
    lams, plain, crossed = [], [], []
    for c in range(per):
        moves = []
        for l in range(nsh):
            s1, s2 = shift(c, l)
            keep = (lane_row >= s1) & (lane_row < PER_TILE + s1)
            moves.append((s1, s2, keep, lane_row < s1, lane_row >= PER_TILE + s1))
        den = load[c, pl.ds(tiles * rows, nb), :].astype(jnp.float32)
        turned = jnp.where(part_im, pltpu.roll(den, nb, 1), -pltpu.roll(den, LANES - nb, 1))
        for f in range(fl):
            re, im = [
                jnp.concatenate([load[c, pl.ds(t * rows + (b * fl + f) * nb, nb), :] for t in range(tiles)], axis=1)
                for b in range(ri)
            ]
            arrived = jnp.concatenate([jnp.concatenate([re, im], axis=1), jnp.concatenate([im, -re], axis=1)], axis=0)
            lams.append(form_factors(cols_ref, moves, c, f, arrived, LANES // nb))
            mine = unit == c * fl + f
            for row_plain, row_crossed in ((den, -turned), (turned, den)):
                plain.append(jnp.where(mine, row_plain, zero))
                crossed.append(jnp.where(mine, row_crossed, zero))
    high, low = split(jnp.concatenate(lams, axis=1))
    mix = jnp.concatenate([jnp.concatenate(plain, axis=0), jnp.concatenate(crossed, axis=0)], axis=1)
    mix = mix.astype(jnp.bfloat16)
    left = jnp.dot(
        jnp.concatenate([high, low], axis=1), jnp.concatenate([mix, mix], axis=0), preferred_element_type=jnp.float32
    )
    lefts, rights = [], []
    for l in range(nsh):
        here = slice(l * nb, (l + 1) * nb)
        scaled = jnp.concatenate([left[here, :LANES], left[here, LANES:]], axis=0) * weight(l)
        s_high, s_low = split(scaled)
        lefts += [s_high, s_high, s_low]
        spread = [
            jnp.concatenate([jnp.where(unit == u, x[here], jnp.zeros_like(x[here])) for u in range(per * fl)], axis=0)
            for x in (high, low)
        ]
        rights += [spread[0], spread[1], spread[0]]
    return nt(jnp.concatenate(lefts, axis=1), jnp.concatenate(rights, axis=1))


def pair_sum(at, shells_ref, weight_ref, shift_x, shift_y, cols, loads, which, kx_count, ky_count):
    per, nsh = cols.shape[2], weight_ref.shape[1]
    total = None
    for load, j in zip(loads, which):
        wrap_x = (at[0] + shift_x[j] >= kx_count).astype(jnp.int32)
        wrap_y = [(at[1] * per + c + shift_y[j] >= per * ky_count).astype(jnp.int32) for c in range(per)]

        def shift(c, l):
            return shells_ref[j, l, 0] + wrap_x, shells_ref[j, l, 1] + wrap_y[c]

        part = transfer_sum(load, cols, shift, lambda l: weight_ref[j, l], nsh)
        total = part if total is None else total + part
    return total


def ready_terms(scalars, vectors, loads, which, kx_count, ky_count):
    ri, _, per, fl, nb, npw = vectors.shape

    def kernel(at, shells_ref, weight_ref, shift_x, shift_y, vec_ref, *refs):
        out_ref, cols = refs[-2:]
        column_shifts(vec_ref, cols)
        out_ref[...] = pair_sum(
            at, shells_ref, weight_ref, shift_x, shift_y, cols, refs[:-2], which, kx_count, ky_count
        )

    return pl.pallas_call(
        kernel,
        in_specs=[SM] * 5 + [VM] * (1 + len(loads)),
        out_specs=VM,
        out_shape=jax.ShapeDtypeStruct((ri * nb, per * fl * nb), jnp.float32),
        scratch_shapes=[pltpu.VMEM((SPAN, ri, per, fl, nb, npw), jnp.bfloat16)],
        compiler_params=params(12),
        name="ready_terms",
    )(*scalars, vectors, *loads)


def last_terms(scalars, vectors, blocks, which, before, kx_count, ky_count, scale):
    ri, _, per, fl, nb, npw = vectors.shape
    count = len(blocks[0])

    def kernel(at, shells_ref, weight_ref, shift_x, shift_y, vec_ref, before_ref, *refs):
        ins, (out_ref, cols, held, sem) = refs[:-4], refs[-4:]
        groups = [ins[i * count : (i + 1) * count] for i in range(len(which))]
        for i, j in enumerate(which):
            start_columns(i, shift_y[j], at[1], groups[i], held.at[i], sem)
        column_shifts(vec_ref, cols)
        for i, j in enumerate(which):
            wait_columns(i, groups[i], held.at[i], sem)
        total = before_ref[...] + pair_sum(
            at, shells_ref, weight_ref, shift_x, shift_y, cols,
            [held.at[i] for i in range(len(which))], which, kx_count, ky_count,
        )
        total = total * scale
        for a in range(ri):
            for c in range(per):
                for f in range(fl):
                    u = c * fl + f
                    out_ref[a, 0, c, f] = total[a * nb : (a + 1) * nb, u * nb : (u + 1) * nb]

    flat = [b for group in blocks for b in group]
    return pl.pallas_call(
        kernel,
        in_specs=[SM] * 5 + [VM, VM] + [ANY] * len(flat),
        out_specs=VM,
        out_shape=jax.ShapeDtypeStruct((ri, 1, per, fl, nb, nb), jnp.float32),
        scratch_shapes=[
            pltpu.VMEM((SPAN, ri, per, fl, nb, npw), jnp.bfloat16),
            pltpu.VMEM((len(which),) + flat[0].shape, flat[0].dtype),
            pltpu.SemaphoreType.DMA((len(which), per)),
        ],
        compiler_params=params(12),
        name="last_terms",
    )(*scalars, vectors, before, *flat)


def body(vectors, density, coulomb, shells, shift_x, shift_y):
    kx_count, ky_count = lax.axis_size("kx"), lax.axis_size("ky")
    transfers, nsh = coulomb.shape
    half = transfers // 2
    gathered, carried = range(half), range(half, transfers)
    at = jnp.stack([lax.axis_index("kx"), lax.axis_index("ky")]).astype(jnp.int32)
    scalars = (at, shells, coulomb, shift_x, shift_y)

    own = pack(vectors, density)
    blocks = [own] + [across_ky(own, ky_count, by) for by in range(1, ky_count)]
    moved = along_kx([own] * half, [shift_x[j] for j in carried], kx_count, ky_count)
    loads = select(at, shift_y, blocks, gathered)
    far = ky_count // 2
    crossed = [across_ky(x, ky_count, far) for x in moved]
    loads = along_kx(loads, [shift_x[j] for j in gathered], kx_count, ky_count)
    spread = []
    for x, y in zip(moved, crossed):
        group = {0: x, far: y}
        bit = far // 2
        while bit:
            group |= {o ^ bit: across_ky(group[o], ky_count, bit) for o in list(group)}
            bit //= 2
        spread.append([group[o] for o in range(ky_count)])
    before = ready_terms(scalars, vectors, loads, gathered, kx_count, ky_count)
    return last_terms(
        scalars, vectors, spread, carried, before, kx_count, ky_count, -1.0 / (transfers * nsh)
    )


def solution(mesh):
    placed = (P(None, "kx", "ky"), P(None, "kx", "ky"), P(), P(), P(), P())
    return jax.shard_map(
        body, mesh=mesh, in_specs=placed, out_specs=P(None, "kx", "ky"), check_vma=False
    )
```

```python
import jax
import jax.numpy as jnp
from jax import lax
from jax.experimental import pallas as pl
from jax.experimental.pallas import tpu as pltpu
from jax.sharding import PartitionSpec as P

GA = 16
GB = 16
LANES = 128
SPAN = 4
PER_TILE = LANES // GB
PER_PLANE = GA // PER_TILE
DIRECT = 8
MIB = 1 << 20
VM = pl.BlockSpec(memory_space=pltpu.VMEM)
SM = pl.BlockSpec(memory_space=pltpu.SMEM)
ANY = pl.BlockSpec(memory_space=pl.ANY)
HBM = pl.BlockSpec(memory_space=pltpu.HBM)


def in_hbm(x):
    return pltpu.with_memory_space_constraint(x, pltpu.HBM)


def params(mib):
    return pltpu.CompilerParams(vmem_limit_bytes=mib * MIB)


def stages(kx_count):
    out, place = [], 1
    while place < kx_count:
        left = kx_count // place
        out.append((place, left if left <= DIRECT else 4))
        place *= out[-1][1]
    return out


def plan_width(nsh, per):
    return 2 * nsh + 5 * per


def pack_kernel(
    vec_hbm, den_hbm, shells_hbm, x_hbm, y_hbm, out_ref, plan_ref, *rest, pairs, kx_count, ky_count
):
    branch_refs, (vec_ref, den_ref, shells_ref, shift_x, shift_y, sem) = rest[:-6], rest[-6:]
    given = (x_hbm, y_hbm, shells_hbm, den_hbm, vec_hbm)
    held = (shift_x, shift_y, shells_ref, den_ref, vec_ref)
    copies = [pltpu.make_async_copy(src, dst, sem.at[i]) for i, (src, dst) in enumerate(zip(given, held))]
    for copy in copies:
        copy.start()
    for copy in copies[:3]:
        copy.wait()
    ri, _, per, fl, nb, npw = vec_ref.shape
    transfers, _, nsh = shells_ref.shape
    tiles = npw // LANES
    rows = ri * fl * nb
    row, me = lax.axis_index("kx"), lax.axis_index("ky")
    span = per * ky_count
    slot = 0
    for place, radix in stages(kx_count):
        for a, b in pairs:
            branch_refs[slot][0] = (shift_x[a] // place) % radix * radix + (shift_x[b] // place) % radix
            slot += 1
    for j in range(transfers):
        wrap = (row + shift_x[j] >= kx_count).astype(jnp.int32)
        for l in range(nsh):
            plan_ref[j, l] = shells_ref[j, 0, l] + wrap
            plan_ref[j, nsh + l] = shells_ref[j, 1, l]
        for c in range(per):
            at = 2 * nsh + 5 * c
            col = me * per + c + shift_y[j]
            wanted = lax.rem(col, span)
            plan_ref[j, at] = (col >= span).astype(jnp.int32)
            plan_ref[j, at + 1] = wanted // per
            plan_ref[j, at + 2] = lax.rem(wanted, per)
            wanted = lax.rem((me ^ (ky_count // 2)) * per + c + shift_y[j], span)
            plan_ref[j, at + 3] = wanted // per
            plan_ref[j, at + 4] = lax.rem(wanted, per)
    for copy in copies[3:]:
        copy.wait()
    for c in range(per):
        for a in range(ri):
            for f in range(fl):
                x = vec_ref[a, 0, c, f]
                for t in range(tiles):
                    out_ref[c, pl.ds(t * rows + (a * fl + f) * nb, nb), :] = x[:, t * LANES : (t + 1) * LANES]
        both = [den_ref[a, 0, c, f].astype(jnp.float32) for f in range(fl) for a in range(ri)]
        wide = jnp.concatenate(both * (LANES // (fl * ri * nb)), axis=1)
        out_ref[c, pl.ds(tiles * rows, nb), :] = wide.astype(jnp.bfloat16)


def pack(vectors, density, shells, shift_x, shift_y, pairs, kx_count, ky_count):
    ri, _, per, fl, nb, npw = vectors.shape
    transfers, nsh, _ = shells.shape
    rows = ri * fl * nb * (npw // LANES) + nb
    branches = len(stages(kx_count)) * len(pairs)

    def kernel(*refs):
        pack_kernel(*refs, pairs=pairs, kx_count=kx_count, ky_count=ky_count)

    out = pl.pallas_call(
        kernel,
        in_specs=[HBM] * 5,
        out_specs=[VM, SM] + [SM] * branches,
        out_shape=[
            jax.ShapeDtypeStruct((per, rows, LANES), jnp.bfloat16),
            jax.ShapeDtypeStruct((transfers, plan_width(nsh, per)), jnp.int32),
        ]
        + [jax.ShapeDtypeStruct((1,), jnp.int32)] * branches,
        scratch_shapes=[
            pltpu.VMEM(vectors.shape, vectors.dtype),
            pltpu.VMEM(density.shape, density.dtype),
            pltpu.SMEM((transfers, 2, nsh), shells.dtype),
            pltpu.SMEM(shift_x.shape, shift_x.dtype),
            pltpu.SMEM(shift_y.shape, shift_y.dtype),
            pltpu.SemaphoreType.DMA((5,)),
        ],
        compiler_params=params(4),
        name="pack_columns",
    )(*[in_hbm(x) for x in (vectors, density, jnp.transpose(shells, (0, 2, 1)), shift_x, shift_y)])
    chosen = [x.reshape(()) for x in out[2:]]
    return out[0], out[1], [chosen[i :: len(pairs)] for i in range(len(pairs))]


def copy_column(offset, place, sources, spare, dst, sem):
    for o, source in enumerate(sources):

        @pl.when(offset == o)
        def _():
            pltpu.make_async_copy(source.at[place], dst, sem).start()

    if spare is not None:

        @pl.when(offset >= len(sources))
        def _():
            pltpu.make_async_copy(spare, dst, sem).start()


def select(plan, blocks, gathered, groups, carried, nsh):
    per = blocks[0].shape[0]
    count, near = len(blocks), len(groups[0])

    def kernel(plan_ref, *refs):
        ins, outs, sem = refs[: -len(gathered) - len(carried) - 1], refs[-len(gathered) - len(carried) - 1 : -1], refs[-1]
        me = lax.axis_index("ky")
        for i, j in enumerate(gathered):
            for c in range(per):
                at = 2 * nsh + 5 * c
                copy_column(plan_ref[j, at + 1] ^ me, plan_ref[j, at + 2], ins[:count], None, outs[i].at[c], sem.at[i, c])
        for i, j in enumerate(carried):
            slot = len(gathered) + i
            group = ins[count + near * i : count + near * (i + 1)]
            for c in range(per):
                at = 2 * nsh + 5 * c
                copy_column(
                    plan_ref[j, at + 3] ^ me, plan_ref[j, at + 4], group, group[0].at[c], outs[slot].at[c], sem.at[slot, c]
                )
        for i, out in enumerate(outs):
            for c in range(per):
                pltpu.make_async_copy(ins[0].at[0], out.at[c], sem.at[i, c]).wait()

    flat = [x for group in groups for x in group]
    outs = len(gathered) + len(carried)
    got = pl.pallas_call(
        kernel,
        in_specs=[SM] + [ANY] * (count + len(flat)),
        out_specs=[ANY] * outs,
        out_shape=[jax.ShapeDtypeStruct(blocks[0].shape, blocks[0].dtype)] * outs,
        scratch_shapes=[pltpu.SemaphoreType.DMA((outs, per))],
        compiler_params=params(1),
        name="select_columns",
    )(plan, *blocks, *flat)
    return got[: len(gathered)], got[len(gathered) :]


def along_kx(parts, chosen, kx_count, ky_count):
    def moved(part, dx):
        if dx % kx_count == 0:
            return part
        pairs = [
            (((x + dx) % kx_count) * ky_count + y, x * ky_count + y) for x in range(kx_count) for y in range(ky_count)
        ]
        return lax.ppermute(part, ("kx", "ky"), pairs)

    for (place, radix), index in zip(stages(kx_count), chosen):

        def branch(a, b):
            return lambda x, y: (moved(x, a * place), moved(y, b * place))

        parts = lax.switch(index, [branch(a, b) for a in range(radix) for b in range(radix)], *parts)
    return parts


def across_ky(part, count, by):
    return lax.ppermute(part, "ky", [(i, i ^ by) for i in range(count)])


def column_shifts(vec_ref, cols_ref):
    ri, _, per, fl, nb, npw = vec_ref.shape
    col = lax.broadcasted_iota(jnp.int32, (nb, LANES), 1) % GB
    for a in range(ri):
        for c in range(per):
            for f in range(fl):
                for t in range(npw // LANES):
                    x = vec_ref[a, 0, c, f, :, t * LANES : (t + 1) * LANES]
                    for s2 in range(-1, SPAN - 1):
                        good = (col >= s2) & (col < GB + s2)
                        y = jnp.where(good, pltpu.roll(x, s2 % LANES, 1), jnp.zeros_like(x)) if s2 else x
                        cols_ref[s2 + 1, a, c, f, :, t * LANES : (t + 1) * LANES] = y


def row_shifted(tiles, s1, keep, above, below, zero):
    moved = [pltpu.roll(x, ((s1 + PER_TILE) % PER_TILE) * GB, 1) for x in tiles]
    out = []
    for t, x in enumerate(moved):
        other = zero
        if t % PER_PLANE > 0:
            other = jnp.where(above, moved[t - 1], other)
        if t % PER_PLANE < PER_PLANE - 1:
            other = jnp.where(below, moved[t + 1], other)
        out.append(jnp.where(keep, x, other))
    return out


def split(x):
    high = x.astype(jnp.bfloat16)
    return high, (x - high.astype(jnp.float32)).astype(jnp.bfloat16)


def nt(a, b):
    return lax.dot_general(a, b, (((1,), (1,)), ((), ())), preferred_element_type=jnp.float32)


def form_factors(cols_ref, moves, c, f, arrived, slots):
    _, ri, _, _, nb, npw = cols_ref.shape
    tiles = npw // LANES
    zero = jnp.zeros((nb, LANES), jnp.bfloat16)
    total = None
    for a in range(ri):
        own = []
        for s1, s2, keep, above, below in moves:
            slab = cols_ref[s2 + 1, a, c, f]
            pieces = [slab[:, t * LANES : (t + 1) * LANES] for t in range(tiles)]
            own.append(row_shifted(pieces, s1, keep, above, below, zero))
        own += [[zero] * tiles] * (slots - len(moves))
        for t in range(0, tiles, PER_PLANE):
            left = jnp.concatenate([jnp.concatenate(o[t : t + PER_PLANE], axis=1) for o in own], axis=0)
            at = a * npw + t * LANES
            part = nt(left, arrived[:, at : at + PER_PLANE * LANES])
            total = part if total is None else total + part
    return total


def transfer_sum(load, cols_ref, shift, weight, nsh):
    _, ri, per, fl, nb, npw = cols_ref.shape
    tiles = npw // LANES
    rows = ri * fl * nb
    lane = lax.broadcasted_iota(jnp.int32, (nb, LANES), 1)
    lane_row = lane // GB
    part_im = (lane // nb) % ri == 1
    unit = lane // (ri * nb)
    zero = jnp.zeros((nb, LANES), jnp.float32)
    lams, plain, crossed = [], [], []
    for c in range(per):
        moves = []
        for l in range(nsh):
            s1, s2 = shift(c, l)
            keep = (lane_row >= s1) & (lane_row < PER_TILE + s1)
            moves.append((s1, s2, keep, lane_row < s1, lane_row >= PER_TILE + s1))
        den = load[c, pl.ds(tiles * rows, nb), :].astype(jnp.float32)
        turned = jnp.where(part_im, pltpu.roll(den, nb, 1), -pltpu.roll(den, LANES - nb, 1))
        for f in range(fl):
            re, im = [
                jnp.concatenate([load[c, pl.ds(t * rows + (b * fl + f) * nb, nb), :] for t in range(tiles)], axis=1)
                for b in range(ri)
            ]
            arrived = jnp.concatenate([jnp.concatenate([re, im], axis=1), jnp.concatenate([im, -re], axis=1)], axis=0)
            lams.append(form_factors(cols_ref, moves, c, f, arrived, LANES // nb))
            mine = unit == c * fl + f
            for row_plain, row_crossed in ((den, -turned), (turned, den)):
                plain.append(jnp.where(mine, row_plain, zero))
                crossed.append(jnp.where(mine, row_crossed, zero))
    high, low = split(jnp.concatenate(lams, axis=1))
    mix = jnp.concatenate([jnp.concatenate(plain, axis=0), jnp.concatenate(crossed, axis=0)], axis=1)
    mix = mix.astype(jnp.bfloat16)
    left = jnp.dot(
        jnp.concatenate([high, low], axis=1), jnp.concatenate([mix, mix], axis=0), preferred_element_type=jnp.float32
    )
    lefts, rights = [], []
    for l in range(nsh):
        here = slice(l * nb, (l + 1) * nb)
        scaled = jnp.concatenate([left[here, :LANES], left[here, LANES:]], axis=0) * weight(l)
        s_high, s_low = split(scaled)
        lefts += [s_high, s_high, s_low]
        spread = [
            jnp.concatenate([jnp.where(unit == u, x[here], jnp.zeros_like(x[here])) for u in range(per * fl)], axis=0)
            for x in (high, low)
        ]
        rights += [spread[0], spread[1], spread[0]]
    return nt(jnp.concatenate(lefts, axis=1), jnp.concatenate(rights, axis=1))


def exchange_terms(plan, weights, vectors, loads, gathered, groups, across, carried, scale):
    ri, _, per, fl, nb, npw = vectors.shape
    nsh = weights.shape[1]
    near = len(groups[0])

    def kernel(plan_ref, weight_ref, vec_ref, *refs):
        ins, (out_ref, cols, held, sem) = refs[:-4], refs[-4:]
        ready, rest = ins[: len(loads)], ins[len(loads) :]
        me = lax.axis_index("ky")
        for i, j in enumerate(carried):
            group = rest[i * (near + 1) : (i + 1) * (near + 1)]
            for c in range(per):
                at = 2 * nsh + 5 * c
                copy_column(
                    plan_ref[j, at + 1] ^ me, plan_ref[j, at + 2], group[:near], group[near].at[c], held.at[i, c], sem.at[i, c]
                )
        column_shifts(vec_ref, cols)
        total = None
        for i, j in enumerate(list(gathered) + list(carried)):
            if i < len(ready):
                load = ready[i]
            else:
                load = held.at[i - len(ready)]
                for c in range(per):
                    pltpu.make_async_copy(rest[0].at[0], load.at[c], sem.at[i - len(ready), c]).wait()

            def shift(c, l):
                return plan_ref[j, l], plan_ref[j, nsh + l] + plan_ref[j, 2 * nsh + 5 * c]

            part = transfer_sum(load, cols, shift, lambda l: weight_ref[j, l], nsh)
            total = part if total is None else total + part
        total = total * scale
        for a in range(ri):
            for c in range(per):
                for f in range(fl):
                    u = c * fl + f
                    out_ref[a, 0, c, f] = total[a * nb : (a + 1) * nb, u * nb : (u + 1) * nb]

    flat = [x for group, window in zip(groups, across) for x in list(group) + [window]]
    return pl.pallas_call(
        kernel,
        in_specs=[SM, SM, VM] + [VM] * len(loads) + [ANY] * len(flat),
        out_specs=VM,
        out_shape=jax.ShapeDtypeStruct((ri, 1, per, fl, nb, nb), jnp.float32),
        scratch_shapes=[
            pltpu.VMEM((SPAN, ri, per, fl, nb, npw), jnp.bfloat16),
            pltpu.VMEM((len(carried),) + loads[0].shape, loads[0].dtype),
            pltpu.SemaphoreType.DMA((len(carried), per)),
        ],
        compiler_params=params(12),
        name="exchange_terms",
    )(plan, weights, vectors, *loads, *flat)


def body(vectors, density, coulomb, shells, shift_x, shift_y):
    kx_count, ky_count = lax.axis_size("kx"), lax.axis_size("ky")
    transfers, nsh = coulomb.shape
    half = transfers // 2
    gathered, carried = range(half), range(half, transfers)
    own, plan, chosen = pack(
        vectors, density, shells, shift_x, shift_y, [tuple(carried), tuple(gathered)], kx_count, ky_count
    )
    blocks = [own] + [across_ky(own, ky_count, by) for by in range(1, ky_count)]
    moved = along_kx([own] * half, chosen[0], kx_count, ky_count)
    far = ky_count // 2
    groups = [[x] + [across_ky(x, ky_count, by) for by in range(1, far)] for x in moved]
    loads, windows = select(plan, blocks, gathered, groups, carried, nsh)
    across = [across_ky(x, ky_count, far) for x in windows]
    loads = along_kx(loads, chosen[1], kx_count, ky_count)
    return exchange_terms(
        plan, coulomb, vectors, loads, gathered, groups, across, carried, -1.0 / (transfers * nsh)
    )


def solution(mesh):
    placed = (P(None, "kx", "ky"), P(None, "kx", "ky"), P(), P(), P(), P())
    return jax.shard_map(
        body, mesh=mesh, in_specs=placed, out_specs=P(None, "kx", "ky"), check_vma=False
    )
```

```python
import itertools

import jax
import jax.numpy as jnp
from jax import lax
from jax.experimental import pallas as pl
from jax.experimental.pallas import tpu as pltpu
from jax.sharding import PartitionSpec as P

GA = 16
GB = 16
LANES = 128
SPAN = 4
PER_TILE = LANES // GB
PER_PLANE = GA // PER_TILE
DIRECT = 8
TOGETHER = 3
MIB = 1 << 20
VM = pl.BlockSpec(memory_space=pltpu.VMEM)
SM = pl.BlockSpec(memory_space=pltpu.SMEM)
HBM = pl.BlockSpec(memory_space=pltpu.HBM)


def in_hbm(x):
    return pltpu.with_memory_space_constraint(x, pltpu.HBM)


def params(mib):
    return pltpu.CompilerParams(vmem_limit_bytes=mib * MIB)


def stages(kx_count):
    out, place = [], 1
    while place < kx_count:
        out.append((place, min(4, kx_count // place)))
        place *= out[-1][1]
    return out


def subsets(count):
    out = []
    for size in range(TOGETHER + 1):
        out += sorted(itertools.combinations(range(1, count), size), key=lambda m: m[::-1])
    return out


def binomial(n, k):
    out = 1
    for i in range(k):
        out = out * (n - i) // (i + 1)
    return out


def traced_binomial(n, k):
    out = 1
    for i in range(k):
        out = out * (n - i)
    return lax.div(out, jnp.int32(binomial(k, k) * [1, 1, 2, 6, 24][k]))


WIDTH = 5


def plan_at(nsh, c):
    return 1 + 2 * nsh + WIDTH * c


def pack_kernel(vec_hbm, den_hbm, shells_hbm, x_hbm, y_hbm, out_ref, plan_ref, *rest, kx_count, ky_count):
    branch_refs, (vec_ref, den_ref, shells_ref, shift_x, shift_y, sem) = rest[:-6], rest[-6:]
    given = (x_hbm, y_hbm, shells_hbm, den_hbm, vec_hbm)
    held = (shift_x, shift_y, shells_ref, den_ref, vec_ref)
    copies = [pltpu.make_async_copy(src, dst, sem.at[i]) for i, (src, dst) in enumerate(zip(given, held))]
    for copy in copies:
        copy.start()
    for copy in copies[:3]:
        copy.wait()
    ri, _, per, fl, nb, npw = vec_ref.shape
    transfers, _, nsh = shells_ref.shape
    tiles = npw // LANES
    rows = ri * fl * nb
    row, me = lax.axis_index("kx"), lax.axis_index("ky")
    span = per * ky_count
    steps = [shift_x[j] for j in range(transfers)]
    if kx_count <= DIRECT:
        order = [jnp.int32(0)] * kx_count
        found = jnp.int32(0)
        members = [jnp.int32(0)] * transfers
        for d in range(1, kx_count):
            used = steps[0] == d
            for q in steps[1:]:
                used = used | (q == d)
            for i in range(transfers):
                members[i] = jnp.where(used & (found == i), d, members[i])
            found = found + used.astype(jnp.int32)
            order[d] = found
        size = jnp.minimum(found, TOGETHER)
        index = jnp.int32(0)
        for i in range(TOGETHER):
            here = size > i
            index = index + jnp.where(here, binomial(kx_count - 1, i), 0)
            index = index + jnp.where(here, traced_binomial(members[i] - 1, i + 1), 0)
        branch_refs[0][0] = index
        for i in range(TOGETHER, transfers):
            branch_refs[1 + i - TOGETHER][0] = members[i]
        slots = []
        for q in steps:
            slot = jnp.int32(0)
            for d in range(1, kx_count):
                slot = jnp.where(q == d, order[d], slot)
            slots.append(slot)
    else:
        at = 0
        for place, radix in stages(kx_count):
            for j in range(0, transfers, 2):
                digits = [lax.rem(steps[j + i] // place, radix) for i in range(2)]
                branch_refs[at][0] = digits[0] * radix + digits[1]
                at += 1
        slots = [jnp.int32(j + 1) for j in range(transfers)]
    for j in range(transfers):
        plan_ref[j, 0] = slots[j]
        wrap = (row + steps[j] >= kx_count).astype(jnp.int32)
        for l in range(nsh):
            plan_ref[j, 1 + l] = shells_ref[j, 0, l] + wrap
            plan_ref[j, 1 + nsh + l] = shells_ref[j, 1, l]
        for c in range(per):
            at = plan_at(nsh, c)
            col = me * per + c
            back = lax.rem(col + span - shift_y[j], span)
            plan_ref[j, at] = (back + shift_y[j] >= span).astype(jnp.int32)
            plan_ref[j, at + 1] = (back // per) ^ me
            plan_ref[j, at + 2] = lax.rem(back, per)
            ahead = lax.rem(col + shift_y[j], span)
            plan_ref[j, at + 3] = (ahead // per) ^ me
            plan_ref[j, at + 4] = lax.rem(ahead, per)
    for copy in copies[3:]:
        copy.wait()
    for c in range(per):
        for a in range(ri):
            for f in range(fl):
                x = vec_ref[a, 0, c, f]
                for t in range(tiles):
                    out_ref[c, pl.ds(t * rows + (a * fl + f) * nb, nb), :] = x[:, t * LANES : (t + 1) * LANES]
        both = [den_ref[a, 0, c, f].astype(jnp.float32) for f in range(fl) for a in range(ri)]
        wide = jnp.concatenate(both * (LANES // (fl * ri * nb)), axis=1)
        out_ref[c, pl.ds(tiles * rows, nb), :] = wide.astype(jnp.bfloat16)


def pack(vectors, density, shells, shift_x, shift_y, kx_count, ky_count):
    ri, _, per, fl, nb, npw = vectors.shape
    transfers, nsh, _ = shells.shape
    rows = ri * fl * nb * (npw // LANES) + nb
    if kx_count <= DIRECT:
        branches = 1 + max(transfers - TOGETHER, 0)
    else:
        branches = len(stages(kx_count)) * transfers // 2

    def kernel(*refs):
        pack_kernel(*refs, kx_count=kx_count, ky_count=ky_count)

    out = pl.pallas_call(
        kernel,
        in_specs=[HBM] * 5,
        out_specs=[VM, SM] + [SM] * branches,
        out_shape=[
            jax.ShapeDtypeStruct((per, rows, LANES), jnp.bfloat16),
            jax.ShapeDtypeStruct((transfers, plan_at(nsh, per)), jnp.int32),
        ]
        + [jax.ShapeDtypeStruct((1,), jnp.int32)] * branches,
        scratch_shapes=[
            pltpu.VMEM(vectors.shape, vectors.dtype),
            pltpu.VMEM(density.shape, density.dtype),
            pltpu.SMEM((transfers, 2, nsh), shells.dtype),
            pltpu.SMEM(shift_x.shape, shift_x.dtype),
            pltpu.SMEM(shift_y.shape, shift_y.dtype),
            pltpu.SemaphoreType.DMA((5,)),
        ],
        compiler_params=params(4),
        name="pack_columns",
    )(*[in_hbm(x) for x in (vectors, density, jnp.transpose(shells, (0, 2, 1)), shift_x, shift_y)])
    return out[0], out[1], [x.reshape(()) for x in out[2:]]


def arrivals(own, chosen, transfers, kx_count, ky_count):
    def moved(part, dx):
        pairs = [
            (((x + dx) % kx_count) * ky_count + y, x * ky_count + y) for x in range(kx_count) for y in range(ky_count)
        ]
        return lax.ppermute(part, ("kx", "ky"), pairs)

    if kx_count <= DIRECT:

        def branch(members, size):
            def move(x):
                out = [moved(x, d) for d in members]
                return tuple(out + [jnp.zeros_like(x)] * (size - len(members)))

            return move

        parts = list(lax.switch(chosen[0], [branch(m, TOGETHER) for m in subsets(kx_count)], own))
        for index in chosen[1:]:
            parts += lax.switch(index, [branch((d,) if d else (), 1) for d in range(kx_count)], own)
        return parts

    parts = [own] * transfers
    at = 0
    for place, radix in stages(kx_count):

        def pair(a, b):
            return lambda x, y: tuple(moved(p, d * place) if d else p for p, d in ((x, a), (y, b)))

        branches = [pair(a, b) for a in range(radix) for b in range(radix)]
        for j in range(0, transfers, 2):
            parts[j : j + 2] = lax.switch(chosen[at], branches, *parts[j : j + 2])
            at += 1
    return parts


def across_ky(part, count, by):
    return lax.ppermute(part, "ky", [(i, i ^ by) for i in range(count)])


def shifted_tiles(tiles, turn, keep, above, below, zero):
    moved = [pltpu.roll(x, turn, 1) for x in tiles]
    out = []
    for t, x in enumerate(moved):
        other = zero
        if t % PER_PLANE > 0:
            other = jnp.where(above, moved[t - 1], other)
        if t % PER_PLANE < PER_PLANE - 1:
            other = jnp.where(below, moved[t + 1], other)
        out.append(jnp.where(keep, x, other))
    return out


def split(x):
    high = x.astype(jnp.bfloat16)
    return high, (x - high.astype(jnp.float32)).astype(jnp.bfloat16)


def nt(a, b):
    return lax.dot_general(a, b, (((1,), (1,)), ((), ())), preferred_element_type=jnp.float32)


def rows_of(ref, c, t, part, f, fl, nb, rows):
    return ref[c, pl.ds(t * rows + (part * fl + f) * nb, nb), :]


def transfer_sum(near_ref, far_ref, shift, weight, dims, nsh):
    ri, per, fl, nb, npw = dims
    tiles = npw // LANES
    rows = ri * fl * nb
    lane = lax.broadcasted_iota(jnp.int32, (nb, LANES), 1)
    lane_row, lane_col = lane // GB, lane % GB
    part_im = (lane // nb) % ri == 1
    unit = lane // (ri * nb)
    zero = jnp.zeros((nb, LANES), jnp.float32)
    none = jnp.zeros((nb, LANES), jnp.bfloat16)
    lams, plain, crossed = [], [], []
    for c in range(per):
        moves = []
        for l in range(nsh):
            s1, s2 = shift(c, l)
            inside = (lane_col >= s2) & (lane_col < GB + s2)
            keep = inside & (lane_row >= s1) & (lane_row < PER_TILE + s1)
            turn = (s1 * GB + s2 + LANES) & (LANES - 1)
            moves.append((turn, keep, inside & (lane_row < s1), inside & (lane_row >= PER_TILE + s1), none))
        den = far_ref[c, pl.ds(tiles * rows, nb), :].astype(jnp.float32)
        turned = jnp.where(part_im, pltpu.roll(den, nb, 1), -pltpu.roll(den, LANES - nb, 1))
        for f in range(fl):
            re, im = [[rows_of(far_ref, c, t, b, f, fl, nb, rows) for t in range(tiles)] for b in range(ri)]
            lam = None
            for a in range(ri):
                pieces = [rows_of(near_ref, c, t, a, f, fl, nb, rows) for t in range(tiles)]
                own = [shifted_tiles(pieces, *m) for m in moves]
                own += [[none] * tiles] * (LANES // nb - nsh)
                for t in range(0, tiles, PER_PLANE):
                    at = range(t, t + PER_PLANE)
                    left = jnp.concatenate([jnp.concatenate([o[i] for i in at], axis=1) for o in own], axis=0)
                    real = jnp.concatenate([(im if a else re)[i] for i in at], axis=1)
                    imag = jnp.concatenate([-re[i] if a else im[i] for i in at], axis=1)
                    part = nt(left, jnp.concatenate([real, imag], axis=0))
                    lam = part if lam is None else lam + part
            lams.append(lam)
            mine = unit == c * fl + f
            for row_plain, row_crossed in ((den, -turned), (turned, den)):
                plain.append(jnp.where(mine, row_plain, zero))
                crossed.append(jnp.where(mine, row_crossed, zero))
    high, low = split(jnp.concatenate(lams, axis=1))
    mix = jnp.concatenate([jnp.concatenate(plain, axis=0), jnp.concatenate(crossed, axis=0)], axis=1)
    mix = mix.astype(jnp.bfloat16)
    left = jnp.dot(
        jnp.concatenate([high, low], axis=1), jnp.concatenate([mix, mix], axis=0), preferred_element_type=jnp.float32
    )
    lefts, rights = [], []
    for l in range(nsh):
        here = slice(l * nb, (l + 1) * nb)
        scaled = jnp.concatenate([left[here, :LANES], left[here, LANES:]], axis=0) * weight(l)
        s_high, s_low = split(scaled)
        lefts += [s_high, s_high, s_low]
        spread = [
            jnp.concatenate([jnp.where(unit == u, x[here], jnp.zeros_like(x[here])) for u in range(per * fl)], axis=0)
            for x in (high, low)
        ]
        rights += [spread[0], spread[1], spread[0]]
    return nt(jnp.concatenate(lefts, axis=1), jnp.concatenate(rights, axis=1))


def terms(plan, weights, blocks, arrived, dims, transfers):
    ri, per, fl, nb, npw = dims
    nsh = weights.shape[1]
    count = len(blocks)
    wide = per * fl * nb

    def kernel(plan_ref, weight_ref, *refs):
        ins, others, (out_ref, near, far) = refs[:count], refs[count:-3], refs[-3:]
        for j in range(transfers):
            for i, source in enumerate((ins[0],) + tuple(others)):

                @pl.when(plan_ref[j, 0] == i)
                def _():
                    far[j] = source[...]

            for c in range(per):
                at = plan_at(nsh, c)
                for o in range(count):

                    @pl.when(plan_ref[j, at + 1] == o)
                    def _():
                        near[j, c] = ins[o][plan_ref[j, at + 2]]

        for j in range(transfers):

            def shift(c, l):
                return plan_ref[j, 1 + l], plan_ref[j, 1 + nsh + l] + plan_ref[j, plan_at(nsh, c)]

            total = transfer_sum(near.at[j], far.at[j], shift, lambda l: weight_ref[j, l], dims, nsh)
            per_row = LANES // wide
            top = (j // per_row) * ri * nb
            left = (j % per_row) * wide
            out_ref[top : top + ri * nb, left : left + wide] = total

    return pl.pallas_call(
        kernel,
        in_specs=[SM, SM] + [VM] * (count + len(arrived)),
        out_specs=VM,
        out_shape=jax.ShapeDtypeStruct((transfers * wide // LANES * ri * nb, LANES), jnp.float32),
        scratch_shapes=[pltpu.VMEM((transfers,) + blocks[0].shape, blocks[0].dtype)] * 2,
        compiler_params=params(16),
        name="exchange_terms",
    )(plan, weights, *blocks, *arrived)


def collect(plan, sums, dims, transfers, nsh, scale):
    ri, per, fl, nb, npw = dims
    count = len(sums)
    wide = per * fl * nb
    per_row = LANES // wide

    def kernel(plan_ref, *refs):
        ins, out_ref = refs[:-1], refs[-1]
        unit = lax.broadcasted_iota(jnp.int32, (ri * nb, LANES), 1) // (fl * nb)
        total = jnp.zeros((ri * nb, LANES), jnp.float32)
        for j in range(transfers):
            top = (j // per_row) * ri * nb
            parts = [x[top : top + ri * nb, :] for x in ins]
            for c in range(per):
                at = plan_at(nsh, c)
                off, place = plan_ref[j, at + 3], plan_ref[j, at + 4]
                part = parts[0]
                for o in range(1, count):
                    part = jnp.where(off == o, parts[o], part)
                turn = (c * fl * nb - (j % per_row) * wide - place * fl * nb) & (LANES - 1)
                total = total + jnp.where(unit == c, pltpu.roll(part, turn, 1), 0.0)
        total = total * scale
        for a in range(ri):
            for c in range(per):
                for f in range(fl):
                    u = c * fl + f
                    out_ref[a, 0, c, f] = total[a * nb : (a + 1) * nb, u * nb : (u + 1) * nb]

    return pl.pallas_call(
        kernel,
        in_specs=[SM] + [VM] * count,
        out_specs=VM,
        out_shape=jax.ShapeDtypeStruct((ri, 1, per, fl, nb, nb), jnp.float32),
        compiler_params=params(2),
        name="collect_terms",
    )(plan, *sums)


def body(vectors, density, coulomb, shells, shift_x, shift_y):
    kx_count, ky_count = lax.axis_size("kx"), lax.axis_size("ky")
    ri, _, per, fl, nb, npw = vectors.shape
    dims = (ri, per, fl, nb, npw)
    transfers, nsh = coulomb.shape
    own, plan, chosen = pack(vectors, density, shells, shift_x, shift_y, kx_count, ky_count)
    blocks = [own] + [across_ky(own, ky_count, by) for by in range(1, ky_count)]
    arrived = arrivals(own, chosen, transfers, kx_count, ky_count)
    part = terms(plan, coulomb, blocks, arrived, dims, transfers)
    sums = [part] + [across_ky(part, ky_count, by) for by in range(1, ky_count)]
    return collect(plan, sums, dims, transfers, nsh, -1.0 / (transfers * nsh))


def solution(mesh):
    placed = (P(None, "kx", "ky"), P(None, "kx", "ky"), P(), P(), P(), P())
    return jax.shard_map(
        body, mesh=mesh, in_specs=placed, out_specs=P(None, "kx", "ky"), check_vma=False
    )
```

```python
import itertools
import math

import jax
import jax.numpy as jnp
from jax import lax
from jax.experimental import pallas as pl
from jax.experimental.pallas import tpu as pltpu
from jax.sharding import PartitionSpec as P

GA = 16
GB = 16
LANES = 128
SPAN = 4
PER_TILE = LANES // GB
PER_PLANE = GA // PER_TILE
DIRECT = 8
TOGETHER = 3
MIB = 1 << 20
VM = pl.BlockSpec(memory_space=pltpu.VMEM)
SM = pl.BlockSpec(memory_space=pltpu.SMEM)
HBM = pl.BlockSpec(memory_space=pltpu.HBM)


def in_hbm(x):
    return pltpu.with_memory_space_constraint(x, pltpu.HBM)


def params(mib):
    return pltpu.CompilerParams(vmem_limit_bytes=mib * MIB)


def stages(kx_count):
    out, place = [], 1
    while place < kx_count:
        out.append((place, min(4, kx_count // place)))
        place *= out[-1][1]
    return out


def subsets(count):
    out = []
    for size in range(TOGETHER + 1):
        out += sorted(itertools.combinations(range(1, count), size), key=lambda m: m[::-1])
    return out


def traced_binomial(n, k):
    out = n
    for i in range(1, k):
        out = out * (n - i)
    return lax.div(out, jnp.int32(math.factorial(k)))


WIDTH = 5


def plan_at(nsh, c):
    return 1 + 2 * nsh + WIDTH * c


def pack_kernel(vec_hbm, den_hbm, shells_hbm, x_hbm, y_hbm, out_ref, plan_ref, *rest, kx_count, ky_count):
    branch_refs, (vec_ref, den_ref, shells_ref, shift_x, shift_y, sem) = rest[:-6], rest[-6:]
    given = (x_hbm, y_hbm, shells_hbm, den_hbm, vec_hbm)
    held = (shift_x, shift_y, shells_ref, den_ref, vec_ref)
    copies = [pltpu.make_async_copy(src, dst, sem.at[i]) for i, (src, dst) in enumerate(zip(given, held))]
    for copy in copies:
        copy.start()
    for copy in copies[:3]:
        copy.wait()
    ri, _, per, fl, nb, npw = vec_ref.shape
    transfers, _, nsh = shells_ref.shape
    tiles = npw // LANES
    rows = ri * fl * nb
    row, me = lax.axis_index("kx"), lax.axis_index("ky")
    span = per * ky_count
    steps = [shift_x[j] for j in range(transfers)]
    if kx_count <= DIRECT:
        order = [jnp.int32(0)] * kx_count
        found = jnp.int32(0)
        members = [jnp.int32(0)] * transfers
        for d in range(1, kx_count):
            used = steps[0] == d
            for q in steps[1:]:
                used = used | (q == d)
            for i in range(transfers):
                members[i] = jnp.where(used & (found == i), d, members[i])
            found = found + used.astype(jnp.int32)
            order[d] = found
        index = jnp.int32(0)
        for i in range(TOGETHER):
            here = found > i
            index = index + jnp.where(here, math.comb(kx_count - 1, i), 0)
            index = index + jnp.where(here, traced_binomial(members[i] - 1, i + 1), 0)
        branch_refs[0][0] = jnp.where(found > TOGETHER, len(subsets(kx_count)), index)
        for i in range(0, transfers, 2):
            index = members[i] + traced_binomial(members[i + 1] - 1, 2)
            branch_refs[1 + i // 2][0] = jnp.where(found > TOGETHER, index - 1, 0)
        slots = []
        for q in steps:
            slot = jnp.int32(0)
            for d in range(1, kx_count):
                slot = jnp.where(q == d, order[d], slot)
            slots.append(slot)
    else:
        at = 0
        for place, radix in stages(kx_count):
            for j in range(0, transfers, 2):
                digits = [lax.rem(steps[j + i] // place, radix) for i in range(2)]
                branch_refs[at][0] = digits[0] * radix + digits[1]
                at += 1
        slots = [jnp.int32(j + 1) for j in range(transfers)]
    for j in range(transfers):
        plan_ref[j, 0] = slots[j]
        wrap = (row + steps[j] >= kx_count).astype(jnp.int32)
        for l in range(nsh):
            plan_ref[j, 1 + l] = shells_ref[j, 0, l] + wrap
            plan_ref[j, 1 + nsh + l] = shells_ref[j, 1, l]
        for c in range(per):
            at = plan_at(nsh, c)
            col = me * per + c
            back = lax.rem(col + span - shift_y[j], span)
            plan_ref[j, at] = (back + shift_y[j] >= span).astype(jnp.int32)
            plan_ref[j, at + 1] = (back // per) ^ me
            plan_ref[j, at + 2] = lax.rem(back, per)
            ahead = lax.rem(col + shift_y[j], span)
            plan_ref[j, at + 3] = (ahead // per) ^ me
            plan_ref[j, at + 4] = lax.rem(ahead, per)
    for copy in copies[3:]:
        copy.wait()
    for c in range(per):
        for a in range(ri):
            for f in range(fl):
                x = vec_ref[a, 0, c, f]
                for t in range(tiles):
                    out_ref[c, pl.ds(t * rows + (a * fl + f) * nb, nb), :] = x[:, t * LANES : (t + 1) * LANES]
        both = [den_ref[a, 0, c, f].astype(jnp.float32) for f in range(fl) for a in range(ri)]
        wide = jnp.concatenate(both * (LANES // (fl * ri * nb)), axis=1)
        out_ref[c, pl.ds(tiles * rows, nb), :] = wide.astype(jnp.bfloat16)


def pack(vectors, density, shells, shift_x, shift_y, kx_count, ky_count):
    ri, _, per, fl, nb, npw = vectors.shape
    transfers, nsh, _ = shells.shape
    rows = ri * fl * nb * (npw // LANES) + nb
    if kx_count <= DIRECT:
        branches = 1 + transfers // 2
    else:
        branches = len(stages(kx_count)) * transfers // 2

    def kernel(*refs):
        pack_kernel(*refs, kx_count=kx_count, ky_count=ky_count)

    out = pl.pallas_call(
        kernel,
        in_specs=[HBM] * 5,
        out_specs=[VM, SM] + [SM] * branches,
        out_shape=[
            jax.ShapeDtypeStruct((per, rows, LANES), jnp.bfloat16),
            jax.ShapeDtypeStruct((transfers, plan_at(nsh, per)), jnp.int32),
        ]
        + [jax.ShapeDtypeStruct((1,), jnp.int32)] * branches,
        scratch_shapes=[
            pltpu.VMEM(vectors.shape, vectors.dtype),
            pltpu.VMEM(density.shape, density.dtype),
            pltpu.SMEM((transfers, 2, nsh), shells.dtype),
            pltpu.SMEM(shift_x.shape, shift_x.dtype),
            pltpu.SMEM(shift_y.shape, shift_y.dtype),
            pltpu.SemaphoreType.DMA((5,)),
        ],
        compiler_params=params(4),
        name="pack_columns",
    )(*[in_hbm(x) for x in (vectors, density, jnp.transpose(shells, (0, 2, 1)), shift_x, shift_y)])
    return out[0], out[1], [x.reshape(()) for x in out[2:]]


def arrivals(own, chosen, transfers, kx_count, ky_count):
    def moved(part, dx):
        pairs = [
            (((x + dx) % kx_count) * ky_count + y, x * ky_count + y) for x in range(kx_count) for y in range(ky_count)
        ]
        return lax.ppermute(part, ("kx", "ky"), pairs)

    if kx_count <= DIRECT:

        def together(members, size):
            def move(x, *_):
                out = [moved(x, d) for d in members]
                return tuple(out + [jnp.zeros_like(x)] * (size - len(members)))

            return move

        def by_pairs(x, *indices):
            pairs = [together(m, 2) for m in subsets(kx_count) if len(m) == 2]
            return sum((tuple(lax.switch(i, pairs, x)) for i in indices), ())

        branches = [together(m, transfers) for m in subsets(kx_count)] + [by_pairs]
        return list(lax.switch(chosen[0], branches, own, *chosen[1:]))

    parts = [own] * transfers
    at = 0
    for place, radix in stages(kx_count):

        def pair(a, b):
            return lambda x, y: tuple(moved(p, d * place) if d else p for p, d in ((x, a), (y, b)))

        branches = [pair(a, b) for a in range(radix) for b in range(radix)]
        for j in range(0, transfers, 2):
            parts[j : j + 2] = lax.switch(chosen[at], branches, *parts[j : j + 2])
            at += 1
    return parts


def across_ky(part, count, by):
    return lax.ppermute(part, "ky", [(i, i ^ by) for i in range(count)])


def shifted_tiles(tiles, turn, keep, above, below, zero):
    moved = [pltpu.roll(x, turn, 1) for x in tiles]
    out = []
    for t, x in enumerate(moved):
        other = zero
        if t % PER_PLANE > 0:
            other = jnp.where(above, moved[t - 1], other)
        if t % PER_PLANE < PER_PLANE - 1:
            other = jnp.where(below, moved[t + 1], other)
        out.append(jnp.where(keep, x, other))
    return out


def split(x):
    high = x.astype(jnp.bfloat16)
    return high, (x - high.astype(jnp.float32)).astype(jnp.bfloat16)


def nt(a, b):
    return lax.dot_general(a, b, (((1,), (1,)), ((), ())), preferred_element_type=jnp.float32)


def rows_of(ref, c, t, part, f, fl, nb, rows):
    return ref[c, pl.ds(t * rows + (part * fl + f) * nb, nb), :]


def transfer_sum(near_ref, far_ref, shift, weight, dims, nsh):
    ri, per, fl, nb, npw = dims
    tiles = npw // LANES
    rows = ri * fl * nb
    lane = lax.broadcasted_iota(jnp.int32, (nb, LANES), 1)
    lane_row, lane_col = lane // GB, lane % GB
    part_im = (lane // nb) % ri == 1
    unit = lane // (ri * nb)
    zero = jnp.zeros((nb, LANES), jnp.float32)
    none = jnp.zeros((nb, LANES), jnp.bfloat16)
    lams, plain, crossed = [], [], []
    for c in range(per):
        moves = []
        for l in range(nsh):
            s1, s2 = shift(c, l)
            inside = (lane_col >= s2) & (lane_col < GB + s2)
            keep = inside & (lane_row >= s1) & (lane_row < PER_TILE + s1)
            turn = (s1 * GB + s2 + LANES) & (LANES - 1)
            moves.append((turn, keep, inside & (lane_row < s1), inside & (lane_row >= PER_TILE + s1), none))
        den = far_ref[c, pl.ds(tiles * rows, nb), :].astype(jnp.float32)
        turned = jnp.where(part_im, pltpu.roll(den, nb, 1), -pltpu.roll(den, LANES - nb, 1))
        for f in range(fl):
            re, im = [[rows_of(far_ref, c, t, b, f, fl, nb, rows) for t in range(tiles)] for b in range(ri)]
            lam = None
            for a in range(ri):
                pieces = [rows_of(near_ref, c, t, a, f, fl, nb, rows) for t in range(tiles)]
                own = [shifted_tiles(pieces, *m) for m in moves]
                own += [[none] * tiles] * (LANES // nb - nsh)
                for t in range(0, tiles, PER_PLANE):
                    at = range(t, t + PER_PLANE)
                    left = jnp.concatenate([jnp.concatenate([o[i] for i in at], axis=1) for o in own], axis=0)
                    real = jnp.concatenate([(im if a else re)[i] for i in at], axis=1)
                    imag = jnp.concatenate([-re[i] if a else im[i] for i in at], axis=1)
                    part = nt(left, jnp.concatenate([real, imag], axis=0))
                    lam = part if lam is None else lam + part
            lams.append(lam)
            mine = unit == c * fl + f
            for row_plain, row_crossed in ((den, -turned), (turned, den)):
                plain.append(jnp.where(mine, row_plain, zero))
                crossed.append(jnp.where(mine, row_crossed, zero))
    high, low = split(jnp.concatenate(lams, axis=1))
    mix = jnp.concatenate([jnp.concatenate(plain, axis=0), jnp.concatenate(crossed, axis=0)], axis=1)
    mix = mix.astype(jnp.bfloat16)
    left = jnp.dot(
        jnp.concatenate([high, low], axis=1), jnp.concatenate([mix, mix], axis=0), preferred_element_type=jnp.float32
    )
    lefts, rights = [], []
    for l in range(nsh):
        here = slice(l * nb, (l + 1) * nb)
        scaled = jnp.concatenate([left[here, :LANES], left[here, LANES:]], axis=0) * weight(l)
        s_high, s_low = split(scaled)
        lefts += [s_high, s_high, s_low]
        spread = [
            jnp.concatenate([jnp.where(unit == u, x[here], jnp.zeros_like(x[here])) for u in range(per * fl)], axis=0)
            for x in (high, low)
        ]
        rights += [spread[0], spread[1], spread[0]]
    return nt(jnp.concatenate(lefts, axis=1), jnp.concatenate(rights, axis=1))


def terms(plan, weights, blocks, arrived, dims, transfers):
    ri, per, fl, nb, npw = dims
    nsh = weights.shape[1]
    count = len(blocks)
    wide = per * fl * nb

    def kernel(plan_ref, weight_ref, *refs):
        ins, others, (out_ref, near, far) = refs[:count], refs[count:-3], refs[-3:]
        for j in range(transfers):
            for i, source in enumerate((ins[0],) + tuple(others)):

                @pl.when(plan_ref[j, 0] == i)
                def _():
                    far[j] = source[...]

            for c in range(per):
                at = plan_at(nsh, c)
                for o in range(count):

                    @pl.when(plan_ref[j, at + 1] == o)
                    def _():
                        near[j, c] = ins[o][plan_ref[j, at + 2]]

        for j in range(transfers):

            def shift(c, l):
                return plan_ref[j, 1 + l], plan_ref[j, 1 + nsh + l] + plan_ref[j, plan_at(nsh, c)]

            total = transfer_sum(near.at[j], far.at[j], shift, lambda l: weight_ref[j, l], dims, nsh)
            per_row = LANES // wide
            top = (j // per_row) * ri * nb
            left = (j % per_row) * wide
            out_ref[top : top + ri * nb, left : left + wide] = total

    return pl.pallas_call(
        kernel,
        in_specs=[SM, SM] + [VM] * (count + len(arrived)),
        out_specs=VM,
        out_shape=jax.ShapeDtypeStruct((transfers * wide // LANES * ri * nb, LANES), jnp.float32),
        scratch_shapes=[pltpu.VMEM((transfers,) + blocks[0].shape, blocks[0].dtype)] * 2,
        compiler_params=params(16),
        name="exchange_terms",
    )(plan, in_hbm(weights), *blocks, *arrived)


def collect(plan, sums, dims, transfers, nsh, scale):
    ri, per, fl, nb, npw = dims
    count = len(sums)
    wide = per * fl * nb
    per_row = LANES // wide

    def kernel(plan_ref, *refs):
        ins, out_ref = refs[:-1], refs[-1]
        unit = lax.broadcasted_iota(jnp.int32, (ri * nb, LANES), 1) // (fl * nb)
        total = jnp.zeros((ri * nb, LANES), jnp.float32)
        for j in range(transfers):
            top = (j // per_row) * ri * nb
            parts = [x[top : top + ri * nb, :] for x in ins]
            for c in range(per):
                at = plan_at(nsh, c)
                off, place = plan_ref[j, at + 3], plan_ref[j, at + 4]
                part = parts[0]
                for o in range(1, count):
                    part = jnp.where(off == o, parts[o], part)
                turn = (c * fl * nb - (j % per_row) * wide - place * fl * nb) & (LANES - 1)
                total = total + jnp.where(unit == c, pltpu.roll(part, turn, 1), 0.0)
        total = total * scale
        for a in range(ri):
            for c in range(per):
                for f in range(fl):
                    u = c * fl + f
                    out_ref[a, 0, c, f] = total[a * nb : (a + 1) * nb, u * nb : (u + 1) * nb]

    return pl.pallas_call(
        kernel,
        in_specs=[SM] + [VM] * count,
        out_specs=VM,
        out_shape=jax.ShapeDtypeStruct((ri, 1, per, fl, nb, nb), jnp.float32),
        compiler_params=params(2),
        name="collect_terms",
    )(plan, *sums)


def body(vectors, density, coulomb, shells, shift_x, shift_y):
    kx_count, ky_count = lax.axis_size("kx"), lax.axis_size("ky")
    ri, _, per, fl, nb, npw = vectors.shape
    dims = (ri, per, fl, nb, npw)
    transfers, nsh = coulomb.shape
    own, plan, chosen = pack(vectors, density, shells, shift_x, shift_y, kx_count, ky_count)
    blocks = [own] + [across_ky(own, ky_count, by) for by in range(1, ky_count)]
    arrived = arrivals(own, chosen, transfers, kx_count, ky_count)
    part = terms(plan, coulomb, blocks, arrived, dims, transfers)
    sums = [part] + [across_ky(part, ky_count, by) for by in range(1, ky_count)]
    return collect(plan, sums, dims, transfers, nsh, -1.0 / (transfers * nsh))


def solution(mesh):
    placed = (P(None, "kx", "ky"), P(None, "kx", "ky"), P(), P(), P(), P())
    return jax.shard_map(
        body, mesh=mesh, in_specs=placed, out_specs=P(None, "kx", "ky"), check_vma=False
    )
```

```python
import itertools
import math
from functools import partial

import jax
import jax.numpy as jnp
from jax import lax
from jax.experimental import pallas as pl
from jax.experimental.pallas import tpu as pltpu
from jax.sharding import PartitionSpec as P

GA = 16
GB = 16
LANES = 128
SPAN = 4
PER_TILE = LANES // GB
PER_PLANE = GA // PER_TILE
DIRECT = 8
TOGETHER = 3
MIB = 1 << 20
VM = pl.BlockSpec(memory_space=pltpu.VMEM)
SM = pl.BlockSpec(memory_space=pltpu.SMEM)
HBM = pl.BlockSpec(memory_space=pltpu.HBM)


def in_hbm(x):
    return pltpu.with_memory_space_constraint(x, pltpu.HBM)


def params(mib):
    return pltpu.CompilerParams(vmem_limit_bytes=mib * MIB)


def stages(kx_count):
    out, place = [], 1
    while place < kx_count:
        out.append((place, min(4, kx_count // place)))
        place *= out[-1][1]
    return out


def subsets(count):
    out = []
    for size in range(TOGETHER + 1):
        out += sorted(itertools.combinations(range(1, count), size), key=lambda m: m[::-1])
    return out


def traced_binomial(n, k):
    out = n
    for i in range(1, k):
        out = out * (n - i)
    return lax.div(out, jnp.int32(math.factorial(k)))


WIDTH = 5


def plan_at(nsh, c):
    return 1 + 2 * nsh + WIDTH * c


def pack_kernel(vec_hbm, den_hbm, shells_hbm, x_hbm, y_hbm, out_ref, plan_ref, *rest, kx_count, ky_count):
    branch_refs, (vec_ref, den_ref, shells_ref, shift_x, shift_y, sem) = rest[:-6], rest[-6:]
    given = (x_hbm, y_hbm, shells_hbm, den_hbm, vec_hbm)
    held = (shift_x, shift_y, shells_ref, den_ref, vec_ref)
    copies = [pltpu.make_async_copy(src, dst, sem.at[i]) for i, (src, dst) in enumerate(zip(given, held))]
    for copy in copies:
        copy.start()
    for copy in copies[:3]:
        copy.wait()
    ri, _, per, fl, nb, npw = vec_ref.shape
    transfers, _, nsh = shells_ref.shape
    tiles = npw // LANES
    rows = ri * fl * nb
    row, me = lax.axis_index("kx"), lax.axis_index("ky")
    span = per * ky_count
    steps = [shift_x[j] for j in range(transfers)]
    if kx_count <= DIRECT:
        order = [jnp.int32(0)] * kx_count
        found = jnp.int32(0)
        members = [jnp.int32(0)] * transfers
        for d in range(1, kx_count):
            used = steps[0] == d
            for q in steps[1:]:
                used = used | (q == d)
            for i in range(transfers):
                members[i] = jnp.where(used & (found == i), d, members[i])
            found = found + used.astype(jnp.int32)
            order[d] = found
        index = jnp.int32(0)
        for i in range(TOGETHER):
            here = found > i
            index = index + jnp.where(here, math.comb(kx_count - 1, i), 0)
            index = index + jnp.where(here, traced_binomial(members[i] - 1, i + 1), 0)
        branch_refs[0][0] = jnp.where(found > TOGETHER, len(subsets(kx_count)), index)
        for i in range(transfers):
            branch_refs[1 + i][0] = jnp.where(found > TOGETHER, members[i] - 1 - i, 0)
        slots = []
        for q in steps:
            slot = jnp.int32(0)
            for d in range(1, kx_count):
                slot = jnp.where(q == d, order[d], slot)
            slots.append(slot)
    else:
        at = 0
        for place, radix in stages(kx_count):
            for j in range(0, transfers, 2):
                digits = [lax.rem(steps[j + i] // place, radix) for i in range(2)]
                branch_refs[at][0] = digits[0] * radix + digits[1]
                at += 1
        slots = [jnp.int32(j + 1) for j in range(transfers)]
    for j in range(transfers):
        plan_ref[j, 0] = slots[j]
        wrap = (row + steps[j] >= kx_count).astype(jnp.int32)
        for l in range(nsh):
            plan_ref[j, 1 + l] = shells_ref[j, 0, l] + wrap
            plan_ref[j, 1 + nsh + l] = shells_ref[j, 1, l]
        for c in range(per):
            at = plan_at(nsh, c)
            col = me * per + c
            back = lax.rem(col + span - shift_y[j], span)
            plan_ref[j, at] = (back + shift_y[j] >= span).astype(jnp.int32)
            plan_ref[j, at + 1] = (back // per) ^ me
            plan_ref[j, at + 2] = lax.rem(back, per)
            ahead = lax.rem(col + shift_y[j], span)
            plan_ref[j, at + 3] = (ahead // per) ^ me
            plan_ref[j, at + 4] = lax.rem(ahead, per)
    for copy in copies[3:]:
        copy.wait()
    for c in range(per):
        for a in range(ri):
            for f in range(fl):
                x = vec_ref[a, 0, c, f]
                for t in range(tiles):
                    out_ref[c, pl.ds(t * rows + (a * fl + f) * nb, nb), :] = x[:, t * LANES : (t + 1) * LANES]
        both = [den_ref[a, 0, c, f].astype(jnp.float32) for f in range(fl) for a in range(ri)]
        wide = jnp.concatenate(both * (LANES // (fl * ri * nb)), axis=1)
        out_ref[c, pl.ds(tiles * rows, nb), :] = wide.astype(jnp.bfloat16)


def pack(vectors, density, shells, shift_x, shift_y, kx_count, ky_count):
    ri, _, per, fl, nb, npw = vectors.shape
    transfers, nsh, _ = shells.shape
    rows = ri * fl * nb * (npw // LANES) + nb
    if kx_count <= DIRECT:
        branches = 1 + transfers
    else:
        branches = len(stages(kx_count)) * transfers // 2

    def kernel(*refs):
        pack_kernel(*refs, kx_count=kx_count, ky_count=ky_count)

    out = pl.pallas_call(
        kernel,
        in_specs=[HBM] * 5,
        out_specs=[VM, SM] + [SM] * branches,
        out_shape=[
            jax.ShapeDtypeStruct((per, rows, LANES), jnp.bfloat16),
            jax.ShapeDtypeStruct((transfers, plan_at(nsh, per)), jnp.int32),
        ]
        + [jax.ShapeDtypeStruct((1,), jnp.int32)] * branches,
        scratch_shapes=[
            pltpu.VMEM(vectors.shape, vectors.dtype),
            pltpu.VMEM(density.shape, density.dtype),
            pltpu.SMEM((transfers, 2, nsh), shells.dtype),
            pltpu.SMEM(shift_x.shape, shift_x.dtype),
            pltpu.SMEM(shift_y.shape, shift_y.dtype),
            pltpu.SemaphoreType.DMA((5,)),
        ],
        compiler_params=params(4),
        name="pack_columns",
    )(*[in_hbm(x) for x in (vectors, density, jnp.transpose(shells, (0, 2, 1)), shift_x, shift_y)])
    return out[0], out[1], [x.reshape(()) for x in out[2:]]


def arrivals(own, chosen, transfers, kx_count, ky_count):
    def moved(part, dx):
        pairs = [
            (((x + dx) % kx_count) * ky_count + y, x * ky_count + y) for x in range(kx_count) for y in range(ky_count)
        ]
        return lax.ppermute(part, ("kx", "ky"), pairs)

    if kx_count <= DIRECT:

        def together(members):
            return lambda x, *_: tuple([moved(x, d) for d in members] + [x] * (transfers - len(members)))

        def singly(x, *indices):
            spare = kx_count - transfers
            return tuple(
                lax.switch(index, [partial(moved, dx=1 + i + d) for d in range(spare)], x)
                for i, index in enumerate(indices)
            )

        branches = [together(m) for m in subsets(kx_count)]
        if kx_count - 1 > TOGETHER:
            branches.append(singly)
        return list(lax.switch(chosen[0], branches, own, *chosen[1:]))

    parts = [own] * transfers
    at = 0
    for place, radix in stages(kx_count):

        def pair(a, b):
            return lambda x, y: tuple(moved(p, d * place) if d else p for p, d in ((x, a), (y, b)))

        branches = [pair(a, b) for a in range(radix) for b in range(radix)]
        for j in range(0, transfers, 2):
            parts[j : j + 2] = lax.switch(chosen[at], branches, *parts[j : j + 2])
            at += 1
    return parts


def across_ky(part, count, by):
    return lax.ppermute(part, "ky", [(i, i ^ by) for i in range(count)])


def shifted_tiles(tiles, turn, keep, above, below, zero):
    moved = [pltpu.roll(x, turn, 1) for x in tiles]
    out = []
    for t, x in enumerate(moved):
        other = zero
        if t % PER_PLANE > 0:
            other = jnp.where(above, moved[t - 1], other)
        if t % PER_PLANE < PER_PLANE - 1:
            other = jnp.where(below, moved[t + 1], other)
        out.append(jnp.where(keep, x, other))
    return out


def split(x):
    high = x.astype(jnp.bfloat16)
    return high, (x - high.astype(jnp.float32)).astype(jnp.bfloat16)


def nt(a, b):
    return lax.dot_general(a, b, (((1,), (1,)), ((), ())), preferred_element_type=jnp.float32)


def rows_of(ref, c, t, part, f, fl, nb, rows):
    return ref[c, pl.ds(t * rows + (part * fl + f) * nb, nb), :]


def transfer_sum(near_ref, far_ref, shift, weight, dims, nsh):
    ri, per, fl, nb, npw = dims
    tiles = npw // LANES
    rows = ri * fl * nb
    lane = lax.broadcasted_iota(jnp.int32, (nb, LANES), 1)
    lane_row, lane_col = lane // GB, lane % GB
    part_im = (lane // nb) % ri == 1
    unit = lane // (ri * nb)
    zero = jnp.zeros((nb, LANES), jnp.float32)
    none = jnp.zeros((nb, LANES), jnp.bfloat16)
    lams, plain, crossed = [], [], []
    for c in range(per):
        moves = []
        for l in range(nsh):
            s1, s2 = shift(c, l)
            inside = (lane_col >= s2) & (lane_col < GB + s2)
            keep = inside & (lane_row >= s1) & (lane_row < PER_TILE + s1)
            turn = (s1 * GB + s2 + LANES) & (LANES - 1)
            moves.append((turn, keep, inside & (lane_row < s1), inside & (lane_row >= PER_TILE + s1), none))
        den = far_ref[c, pl.ds(tiles * rows, nb), :].astype(jnp.float32)
        turned = jnp.where(part_im, pltpu.roll(den, nb, 1), -pltpu.roll(den, LANES - nb, 1))
        for f in range(fl):
            re, im = [[rows_of(far_ref, c, t, b, f, fl, nb, rows) for t in range(tiles)] for b in range(ri)]
            lam = None
            for a in range(ri):
                pieces = [rows_of(near_ref, c, t, a, f, fl, nb, rows) for t in range(tiles)]
                own = [shifted_tiles(pieces, *m) for m in moves]
                own += [[none] * tiles] * (LANES // nb - nsh)
                for t in range(0, tiles, PER_PLANE):
                    at = range(t, t + PER_PLANE)
                    left = jnp.concatenate([jnp.concatenate([o[i] for i in at], axis=1) for o in own], axis=0)
                    real = jnp.concatenate([(im if a else re)[i] for i in at], axis=1)
                    imag = jnp.concatenate([-re[i] if a else im[i] for i in at], axis=1)
                    part = nt(left, jnp.concatenate([real, imag], axis=0))
                    lam = part if lam is None else lam + part
            lams.append(lam)
            mine = unit == c * fl + f
            for row_plain, row_crossed in ((den, -turned), (turned, den)):
                plain.append(jnp.where(mine, row_plain, zero))
                crossed.append(jnp.where(mine, row_crossed, zero))
    high, low = split(jnp.concatenate(lams, axis=1))
    mix = jnp.concatenate([jnp.concatenate(plain, axis=0), jnp.concatenate(crossed, axis=0)], axis=1)
    mix = mix.astype(jnp.bfloat16)
    left = jnp.dot(
        jnp.concatenate([high, low], axis=1), jnp.concatenate([mix, mix], axis=0), preferred_element_type=jnp.float32
    )
    lefts, rights = [], []
    for l in range(nsh):
        here = slice(l * nb, (l + 1) * nb)
        scaled = jnp.concatenate([left[here, :LANES], left[here, LANES:]], axis=0) * weight(l)
        s_high, s_low = split(scaled)
        lefts += [s_high, s_high, s_low]
        spread = [
            jnp.concatenate([jnp.where(unit == u, x[here], jnp.zeros_like(x[here])) for u in range(per * fl)], axis=0)
            for x in (high, low)
        ]
        rights += [spread[0], spread[1], spread[0]]
    return nt(jnp.concatenate(lefts, axis=1), jnp.concatenate(rights, axis=1))


def terms(plan, weights, blocks, arrived, dims, transfers):
    ri, per, fl, nb, npw = dims
    nsh = weights.shape[1]
    count = len(blocks)
    wide = per * fl * nb

    def kernel(plan_ref, weight_ref, *refs):
        ins, others, (out_ref, near, far) = refs[:count], refs[count:-3], refs[-3:]
        for j in range(transfers):
            for i, source in enumerate((ins[0],) + tuple(others)):

                @pl.when(plan_ref[j, 0] == i)
                def _():
                    far[j] = source[...]

            for c in range(per):
                at = plan_at(nsh, c)
                for o in range(count):

                    @pl.when(plan_ref[j, at + 1] == o)
                    def _():
                        near[j, c] = ins[o][plan_ref[j, at + 2]]

        for j in range(transfers):

            def shift(c, l):
                return plan_ref[j, 1 + l], plan_ref[j, 1 + nsh + l] + plan_ref[j, plan_at(nsh, c)]

            total = transfer_sum(near.at[j], far.at[j], shift, lambda l: weight_ref[j, l], dims, nsh)
            per_row = LANES // wide
            top = (j // per_row) * ri * nb
            left = (j % per_row) * wide
            out_ref[top : top + ri * nb, left : left + wide] = total

    return pl.pallas_call(
        kernel,
        in_specs=[SM, SM] + [VM] * (count + len(arrived)),
        out_specs=VM,
        out_shape=jax.ShapeDtypeStruct((transfers * wide // LANES * ri * nb, LANES), jnp.float32),
        scratch_shapes=[pltpu.VMEM((transfers,) + blocks[0].shape, blocks[0].dtype)] * 2,
        compiler_params=params(16),
        name="exchange_terms",
    )(plan, in_hbm(weights), *blocks, *arrived)


def collect(plan, sums, dims, transfers, nsh, scale):
    ri, per, fl, nb, npw = dims
    count = len(sums)
    wide = per * fl * nb
    per_row = LANES // wide

    def kernel(plan_ref, *refs):
        ins, out_ref = refs[:-1], refs[-1]
        unit = lax.broadcasted_iota(jnp.int32, (ri * nb, LANES), 1) // (fl * nb)
        total = jnp.zeros((ri * nb, LANES), jnp.float32)
        for j in range(transfers):
            top = (j // per_row) * ri * nb
            parts = [x[top : top + ri * nb, :] for x in ins]
            for c in range(per):
                at = plan_at(nsh, c)
                off, place = plan_ref[j, at + 3], plan_ref[j, at + 4]
                part = parts[0]
                for o in range(1, count):
                    part = jnp.where(off == o, parts[o], part)
                turn = (c * fl * nb - (j % per_row) * wide - place * fl * nb) & (LANES - 1)
                total = total + jnp.where(unit == c, pltpu.roll(part, turn, 1), 0.0)
        total = total * scale
        for a in range(ri):
            for c in range(per):
                for f in range(fl):
                    u = c * fl + f
                    out_ref[a, 0, c, f] = total[a * nb : (a + 1) * nb, u * nb : (u + 1) * nb]

    return pl.pallas_call(
        kernel,
        in_specs=[SM] + [VM] * count,
        out_specs=VM,
        out_shape=jax.ShapeDtypeStruct((ri, 1, per, fl, nb, nb), jnp.float32),
        compiler_params=params(2),
        name="collect_terms",
    )(plan, *sums)


def body(vectors, density, coulomb, shells, shift_x, shift_y):
    kx_count, ky_count = lax.axis_size("kx"), lax.axis_size("ky")
    ri, _, per, fl, nb, npw = vectors.shape
    dims = (ri, per, fl, nb, npw)
    transfers, nsh = coulomb.shape
    own, plan, chosen = pack(vectors, density, shells, shift_x, shift_y, kx_count, ky_count)
    blocks = [own] + [across_ky(own, ky_count, by) for by in range(1, ky_count)]
    arrived = arrivals(own, chosen, transfers, kx_count, ky_count)
    part = terms(plan, coulomb, blocks, arrived, dims, transfers)
    sums = [part] + [across_ky(part, ky_count, by) for by in range(1, ky_count)]
    return collect(plan, sums, dims, transfers, nsh, -1.0 / (transfers * nsh))


def solution(mesh):
    placed = (P(None, "kx", "ky"), P(None, "kx", "ky"), P(), P(), P(), P())
    return jax.shard_map(
        body, mesh=mesh, in_specs=placed, out_specs=P(None, "kx", "ky"), check_vma=False
    )
```

```python
import itertools
import math
from functools import partial

import jax
import jax.numpy as jnp
from jax import lax
from jax.experimental import pallas as pl
from jax.experimental.pallas import tpu as pltpu
from jax.sharding import PartitionSpec as P

GA = 16
GB = 16
LANES = 128
SPAN = 4
PER_TILE = LANES // GB
PER_PLANE = GA // PER_TILE
DIRECT = 8
TOGETHER = 3
MIB = 1 << 20
VM = pl.BlockSpec(memory_space=pltpu.VMEM)
SM = pl.BlockSpec(memory_space=pltpu.SMEM)
HBM = pl.BlockSpec(memory_space=pltpu.HBM)


def in_hbm(x):
    return pltpu.with_memory_space_constraint(x, pltpu.HBM)


def params(mib):
    return pltpu.CompilerParams(vmem_limit_bytes=mib * MIB)


def stages(kx_count):
    out, place = [], 1
    while place < kx_count:
        out.append((place, min(4, kx_count // place)))
        place *= out[-1][1]
    return out


def subsets(count):
    out = []
    for size in range(TOGETHER + 1):
        out += sorted(itertools.combinations(range(1, count), size), key=lambda m: m[::-1])
    return out


def traced_binomial(n, k):
    out = n
    for i in range(1, k):
        out = out * (n - i)
    return lax.div(out, jnp.int32(math.factorial(k)))


WIDTH = 5


def plan_at(nsh, c):
    return 1 + 2 * nsh + WIDTH * c


def pack_kernel(vec_hbm, den_hbm, shells_hbm, x_hbm, y_hbm, out_ref, plan_ref, *rest, kx_count, ky_count):
    branch_refs, (vec_ref, den_ref, shells_ref, shift_x, shift_y, sem) = rest[:-6], rest[-6:]
    given = (x_hbm, y_hbm, shells_hbm, den_hbm, vec_hbm)
    held = (shift_x, shift_y, shells_ref, den_ref, vec_ref)
    copies = [pltpu.make_async_copy(src, dst, sem.at[i]) for i, (src, dst) in enumerate(zip(given, held))]
    for copy in copies:
        copy.start()
    for copy in copies[:3]:
        copy.wait()
    ri, _, per, fl, nb, npw = vec_ref.shape
    transfers, _, nsh = shells_ref.shape
    row, me = lax.axis_index("kx"), lax.axis_index("ky")
    span = per * ky_count
    steps = [shift_x[j] for j in range(transfers)]
    if kx_count <= DIRECT:
        order = [jnp.int32(0)] * kx_count
        found = jnp.int32(0)
        members = [jnp.int32(0)] * transfers
        for d in range(1, kx_count):
            used = steps[0] == d
            for q in steps[1:]:
                used = used | (q == d)
            for i in range(transfers):
                members[i] = jnp.where(used & (found == i), d, members[i])
            found = found + used.astype(jnp.int32)
            order[d] = found
        index = jnp.int32(0)
        for i in range(TOGETHER):
            here = found > i
            index = index + jnp.where(here, math.comb(kx_count - 1, i), 0)
            index = index + jnp.where(here, traced_binomial(members[i] - 1, i + 1), 0)
        branch_refs[0][0] = jnp.where(found > TOGETHER, len(subsets(kx_count)), index)
        for i in range(transfers):
            branch_refs[1 + i][0] = jnp.where(found > TOGETHER, members[i] - 1 - i, 0)
        slots = []
        for q in steps:
            slot = jnp.int32(0)
            for d in range(1, kx_count):
                slot = jnp.where(q == d, order[d], slot)
            slots.append(slot)
    else:
        at = 0
        for place, radix in stages(kx_count):
            for j in range(0, transfers, 2):
                digits = [lax.rem(steps[j + i] // place, radix) for i in range(2)]
                branch_refs[at][0] = digits[0] * radix + digits[1]
                at += 1
        slots = [jnp.int32(j + 1) for j in range(transfers)]
    for j in range(transfers):
        plan_ref[j, 0] = slots[j]
        wrap = (row + steps[j] >= kx_count).astype(jnp.int32)
        for l in range(nsh):
            plan_ref[j, 1 + l] = shells_ref[j, 0, l] + wrap
            plan_ref[j, 1 + nsh + l] = shells_ref[j, 1, l]
        for c in range(per):
            at = plan_at(nsh, c)
            col = me * per + c
            back = lax.rem(col + span - shift_y[j], span)
            plan_ref[j, at] = (back + shift_y[j] >= span).astype(jnp.int32)
            plan_ref[j, at + 1] = (back // per) ^ me
            plan_ref[j, at + 2] = lax.rem(back, per)
            ahead = lax.rem(col + shift_y[j], span)
            plan_ref[j, at + 3] = (ahead // per) ^ me
            plan_ref[j, at + 4] = lax.rem(ahead, per)
    for copy in copies[3:]:
        copy.wait()
    units = [(c, f, a) for c in range(per) for f in range(fl) for a in range(ri)]
    for t in range(npw // LANES):
        at = slice(t * LANES, (t + 1) * LANES)
        x = jnp.concatenate([vec_ref[a, 0, c, f, :, at] for c, f, a in units], axis=0)
        out_ref[at, :] = x.T
    wide = jnp.concatenate([den_ref[a, 0, c, f].astype(jnp.float32) for c, f, a in units], axis=1)
    out_ref[pl.ds(npw, nb), :] = wide.astype(jnp.bfloat16)


def pack(vectors, density, shells, shift_x, shift_y, kx_count, ky_count):
    ri, _, per, fl, nb, npw = vectors.shape
    transfers, nsh, _ = shells.shape
    if kx_count <= DIRECT:
        branches = 1 + transfers
    else:
        branches = len(stages(kx_count)) * transfers // 2

    def kernel(*refs):
        pack_kernel(*refs, kx_count=kx_count, ky_count=ky_count)

    out = pl.pallas_call(
        kernel,
        in_specs=[HBM] * 5,
        out_specs=[VM, SM] + [SM] * branches,
        out_shape=[
            jax.ShapeDtypeStruct((npw + nb, LANES), jnp.bfloat16),
            jax.ShapeDtypeStruct((transfers, plan_at(nsh, per)), jnp.int32),
        ]
        + [jax.ShapeDtypeStruct((1,), jnp.int32)] * branches,
        scratch_shapes=[
            pltpu.VMEM(vectors.shape, vectors.dtype),
            pltpu.VMEM(density.shape, density.dtype),
            pltpu.SMEM((transfers, 2, nsh), shells.dtype),
            pltpu.SMEM(shift_x.shape, shift_x.dtype),
            pltpu.SMEM(shift_y.shape, shift_y.dtype),
            pltpu.SemaphoreType.DMA((5,)),
        ],
        compiler_params=params(4),
        name="pack_columns",
    )(*[in_hbm(x) for x in (vectors, density, jnp.transpose(shells, (0, 2, 1)), shift_x, shift_y)])
    return out[0], out[1], [x.reshape(()) for x in out[2:]]


def arrivals(own, chosen, transfers, kx_count, ky_count):
    def moved(part, dx):
        pairs = [
            (((x + dx) % kx_count) * ky_count + y, x * ky_count + y) for x in range(kx_count) for y in range(ky_count)
        ]
        return lax.ppermute(part, ("kx", "ky"), pairs)

    if kx_count <= DIRECT:

        def together(members):
            return lambda x, *_: tuple([moved(x, d) for d in members] + [x] * (transfers - len(members)))

        def singly(x, *indices):
            spare = kx_count - transfers
            return tuple(
                lax.switch(index, [partial(moved, dx=1 + i + d) for d in range(spare)], x)
                for i, index in enumerate(indices)
            )

        branches = [together(m) for m in subsets(kx_count)]
        if kx_count - 1 > TOGETHER:
            branches.append(singly)
        return list(lax.switch(chosen[0], branches, own, *chosen[1:]))

    parts = [own] * transfers
    at = 0
    for place, radix in stages(kx_count):

        def pair(a, b):
            return lambda x, y: tuple(moved(p, d * place) if d else p for p, d in ((x, a), (y, b)))

        branches = [pair(a, b) for a in range(radix) for b in range(radix)]
        for j in range(0, transfers, 2):
            parts[j : j + 2] = lax.switch(chosen[at], branches, *parts[j : j + 2])
            at += 1
    return parts


def across_ky(part, count, by):
    return lax.ppermute(part, "ky", [(i, i ^ by) for i in range(count)])


def shifted_tiles(tiles, turn, keep, above, below, zero):
    moved = [pltpu.roll(x, turn, 1) for x in tiles]
    out = []
    for t, x in enumerate(moved):
        other = zero
        if t % PER_PLANE > 0:
            other = jnp.where(above, moved[t - 1], other)
        if t % PER_PLANE < PER_PLANE - 1:
            other = jnp.where(below, moved[t + 1], other)
        out.append(jnp.where(keep, x, other))
    return out


def split(x):
    high = x.astype(jnp.bfloat16)
    return high, (x - high.astype(jnp.float32)).astype(jnp.bfloat16)


def nt(a, b):
    return lax.dot_general(a, b, (((1,), (1,)), ((), ())), preferred_element_type=jnp.float32)


def transfer_sum(near_ref, far_ref, shift, weight, dims, nsh):
    ri, per, fl, nb, npw = dims
    lane = lax.broadcasted_iota(jnp.int32, (nb, LANES), 1)
    lane_row, lane_col = lane // GB, lane % GB
    unit = lane // (ri * nb)
    long_lane = lax.broadcasted_iota(jnp.int32, (nsh * nb, LANES), 1)
    none = jnp.zeros((nb, LANES), jnp.bfloat16)
    moves = []
    for c in range(per):
        moves.append([])
        for l in range(nsh):
            s1, s2 = shift(c, l)
            inside = (lane_col >= s2) & (lane_col < GB + s2)
            keep = inside & (lane_row >= s1) & (lane_row < PER_TILE + s1)
            turn = (s1 * GB + s2 + LANES) & (LANES - 1)
            moves[c].append((turn, keep, inside & (lane_row < s1), inside & (lane_row >= PER_TILE + s1), none))
    plane = PER_PLANE * LANES
    products = {}
    for at in range(0, npw, plane):
        right = far_ref[at : at + plane, :]
        for c in range(per):
            for f in range(fl):
                for a in range(ri):
                    tiles = [near_ref[a, c, f, :, i : i + LANES] for i in range(at, at + plane, LANES)]
                    own = [jnp.concatenate(shifted_tiles(tiles, *m), axis=1) for m in moves[c]]
                    part = jnp.dot(jnp.concatenate(own, axis=0), right, preferred_element_type=jnp.float32)
                    key = (a, c * fl + f)
                    products[key] = products[key] + part if key in products else part
    merged = []
    for a in range(ri):
        x = products[a, 0]
        for u in range(1, per * fl):
            x = jnp.where(long_lane // (ri * nb) == u, products[a, u], x)
        merged.append(x)
    other = jnp.where(
        (long_lane // nb) % ri == 1, -pltpu.roll(merged[1], nb, 1), pltpu.roll(merged[1], LANES - nb, 1)
    )
    lam = merged[0] + other
    den = far_ref[npw : npw + nb, :].astype(jnp.float32)
    turned = jnp.where((lane // nb) % ri == 1, pltpu.roll(den, nb, 1), -pltpu.roll(den, LANES - nb, 1))
    zero = jnp.zeros((nb, LANES), jnp.float32)
    plain, crossed = [], []
    for u in range(per * fl):
        for row_plain, row_crossed in ((den, -turned), (turned, den)):
            plain.append(jnp.where(unit == u, row_plain, zero))
            crossed.append(jnp.where(unit == u, row_crossed, zero))
    high, low = split(lam)
    mix = jnp.concatenate([jnp.concatenate(plain, axis=0), jnp.concatenate(crossed, axis=0)], axis=1)
    mix = mix.astype(jnp.bfloat16)
    left = jnp.dot(
        jnp.concatenate([high, low], axis=1), jnp.concatenate([mix, mix], axis=0), preferred_element_type=jnp.float32
    )
    lefts, rights = [], []
    for l in range(nsh):
        here = slice(l * nb, (l + 1) * nb)
        scaled = jnp.concatenate([left[here, :LANES], left[here, LANES:]], axis=0) * weight(l)
        s_high, s_low = split(scaled)
        lefts += [s_high, s_high, s_low]
        spread = [
            jnp.concatenate([jnp.where(unit == u, x[here], jnp.zeros_like(x[here])) for u in range(per * fl)], axis=0)
            for x in (high, low)
        ]
        rights += [spread[0], spread[1], spread[0]]
    return nt(jnp.concatenate(lefts, axis=1), jnp.concatenate(rights, axis=1))


def terms(plan, weights, blocks, own, arrived, dims, transfers):
    ri, per, fl, nb, npw = dims
    nsh = weights.shape[1]
    count = len(blocks)
    wide = per * fl * nb

    def kernel(plan_ref, weight_ref, *refs):
        ins, others, (out_ref, near, far) = refs[:count], refs[count:-3], refs[-3:]
        for j in range(transfers):
            for i, source in enumerate(others):

                @pl.when(plan_ref[j, 0] == i)
                def _():
                    far[j] = source[...]

            for c in range(per):
                at = plan_at(nsh, c)
                for o in range(count):

                    @pl.when(plan_ref[j, at + 1] == o)
                    def _():
                        for a in range(ri):
                            near[j, a, c] = ins[o][a, 0, plan_ref[j, at + 2]]

        for j in range(transfers):

            def shift(c, l):
                return plan_ref[j, 1 + l], plan_ref[j, 1 + nsh + l] + plan_ref[j, plan_at(nsh, c)]

            total = transfer_sum(near.at[j], far.at[j], shift, lambda l: weight_ref[j, l], dims, nsh)
            per_row = LANES // wide
            top = (j // per_row) * ri * nb
            left = (j % per_row) * wide
            out_ref[top : top + ri * nb, left : left + wide] = total

    return pl.pallas_call(
        kernel,
        in_specs=[SM, SM] + [VM] * (count + 1 + len(arrived)),
        out_specs=VM,
        out_shape=jax.ShapeDtypeStruct((transfers * wide // LANES * ri * nb, LANES), jnp.float32),
        scratch_shapes=[
            pltpu.VMEM((transfers, ri, per, fl, nb, npw), blocks[0].dtype),
            pltpu.VMEM((transfers,) + arrived[0].shape, arrived[0].dtype),
        ],
        compiler_params=params(16),
        name="exchange_terms",
    )(plan, in_hbm(weights), *blocks, own, *arrived)


def collect(plan, sums, dims, transfers, nsh, scale):
    ri, per, fl, nb, npw = dims
    count = len(sums)
    wide = per * fl * nb
    per_row = LANES // wide

    def kernel(plan_ref, *refs):
        ins, out_ref = refs[:-1], refs[-1]
        unit = lax.broadcasted_iota(jnp.int32, (ri * nb, LANES), 1) // (fl * nb)
        total = jnp.zeros((ri * nb, LANES), jnp.float32)
        for j in range(transfers):
            top = (j // per_row) * ri * nb
            parts = [x[top : top + ri * nb, :] for x in ins]
            for c in range(per):
                at = plan_at(nsh, c)
                off, place = plan_ref[j, at + 3], plan_ref[j, at + 4]
                part = parts[0]
                for o in range(1, count):
                    part = jnp.where(off == o, parts[o], part)
                turn = (c * fl * nb - (j % per_row) * wide - place * fl * nb) & (LANES - 1)
                total = total + jnp.where(unit == c, pltpu.roll(part, turn, 1), 0.0)
        total = total * scale
        for a in range(ri):
            for c in range(per):
                for f in range(fl):
                    u = c * fl + f
                    out_ref[a, 0, c, f] = total[a * nb : (a + 1) * nb, u * nb : (u + 1) * nb]

    return pl.pallas_call(
        kernel,
        in_specs=[SM] + [VM] * count,
        out_specs=VM,
        out_shape=jax.ShapeDtypeStruct((ri, 1, per, fl, nb, nb), jnp.float32),
        compiler_params=params(2),
        name="collect_terms",
    )(plan, *sums)


def body(vectors, density, coulomb, shells, shift_x, shift_y):
    kx_count, ky_count = lax.axis_size("kx"), lax.axis_size("ky")
    ri, _, per, fl, nb, npw = vectors.shape
    dims = (ri, per, fl, nb, npw)
    transfers, nsh = coulomb.shape
    own, plan, chosen = pack(vectors, density, shells, shift_x, shift_y, kx_count, ky_count)
    blocks = [vectors] + [across_ky(vectors, ky_count, by) for by in range(1, ky_count)]
    arrived = arrivals(own, chosen, transfers, kx_count, ky_count)
    part = terms(plan, coulomb, blocks, own, arrived, dims, transfers)
    sums = {by: across_ky(part, ky_count, by) for by in range(ky_count - 1, 0, -1)}
    sums = [part] + [sums[by] for by in range(1, ky_count)]
    return collect(plan, sums, dims, transfers, nsh, -1.0 / (transfers * nsh))


def solution(mesh):
    placed = (P(None, "kx", "ky"), P(None, "kx", "ky"), P(), P(), P(), P())
    return jax.shard_map(
        body, mesh=mesh, in_specs=placed, out_specs=P(None, "kx", "ky"), check_vma=False
    )
```

```python
import itertools
import math
from functools import partial

import jax
import jax.numpy as jnp
from jax import lax
from jax.experimental import pallas as pl
from jax.experimental.pallas import tpu as pltpu
from jax.sharding import PartitionSpec as P

GA = 16
GB = 16
LANES = 128
SPAN = 4
PER_TILE = LANES // GB
PER_PLANE = GA // PER_TILE
DIRECT = 8
BATCH = 4
TOGETHER = 3
MIB = 1 << 20
VM = pl.BlockSpec(memory_space=pltpu.VMEM)
SM = pl.BlockSpec(memory_space=pltpu.SMEM)
HBM = pl.BlockSpec(memory_space=pltpu.HBM)


def in_hbm(x):
    return pltpu.with_memory_space_constraint(x, pltpu.HBM)


def params(mib):
    return pltpu.CompilerParams(vmem_limit_bytes=mib * MIB)


def stages(kx_count):
    out, place = [], 1
    while place < kx_count:
        out.append((place, min(4, kx_count // place)))
        place *= out[-1][1]
    return out


def subsets(count):
    out = []
    for size in range(TOGETHER + 1):
        out += sorted(itertools.combinations(range(1, count), size), key=lambda m: m[::-1])
    return out


def traced_binomial(n, k):
    out = n
    for i in range(1, k):
        out = out * (n - i)
    return lax.div(out, jnp.int32(math.factorial(k)))


WIDTH = 5


def plan_at(nsh, c):
    return 1 + 2 * nsh + WIDTH * c


def pack_kernel(vec_hbm, den_hbm, shells_hbm, x_hbm, y_hbm, out_ref, plan_ref, *rest, kx_count, ky_count):
    branch_refs, (vec_ref, den_ref, shells_ref, shift_x, shift_y, sem) = rest[:-6], rest[-6:]
    given = (x_hbm, y_hbm, shells_hbm, den_hbm, vec_hbm)
    held = (shift_x, shift_y, shells_ref, den_ref, vec_ref)
    copies = [pltpu.make_async_copy(src, dst, sem.at[i]) for i, (src, dst) in enumerate(zip(given, held))]
    for copy in copies:
        copy.start()
    for copy in copies[:3]:
        copy.wait()
    ri, _, per, fl, nb, npw = vec_ref.shape
    transfers, _, nsh = shells_ref.shape
    row, me = lax.axis_index("kx"), lax.axis_index("ky")
    span = per * ky_count
    steps = [shift_x[j] for j in range(transfers)]
    if kx_count <= DIRECT:
        order = [jnp.int32(0)] * kx_count
        found = jnp.int32(0)
        members = [jnp.int32(0)] * transfers
        for d in range(1, kx_count):
            used = steps[0] == d
            for q in steps[1:]:
                used = used | (q == d)
            for i in range(transfers):
                members[i] = jnp.where(used & (found == i), d, members[i])
            found = found + used.astype(jnp.int32)
            order[d] = found
        index = jnp.int32(0)
        for i in range(TOGETHER):
            here = found > i
            index = index + jnp.where(here, math.comb(kx_count - 1, i), 0)
            index = index + jnp.where(here, traced_binomial(members[i] - 1, i + 1), 0)
        branch_refs[0][0] = jnp.where(found > TOGETHER, len(subsets(kx_count)), index)
        for i in range(transfers):
            branch_refs[1 + i][0] = jnp.where(found > TOGETHER, members[i] - 1 - i, 0)
        slots = []
        for q in steps:
            slot = jnp.int32(0)
            for d in range(1, kx_count):
                slot = jnp.where(q == d, order[d], slot)
            slots.append(slot)
    else:
        at = 0
        for place, radix in stages(kx_count):
            for j in range(0, transfers, 2):
                digits = [lax.rem(steps[j + i] // place, radix) for i in range(2)]
                branch_refs[at][0] = digits[0] * radix + digits[1]
                at += 1
        slots = [jnp.int32(j + 1) for j in range(transfers)]
    for j in range(transfers):
        plan_ref[j, 0] = slots[j]
        wrap = (row + steps[j] >= kx_count).astype(jnp.int32)
        for l in range(nsh):
            plan_ref[j, 1 + l] = shells_ref[j, 0, l] + wrap
            plan_ref[j, 1 + nsh + l] = shells_ref[j, 1, l]
        for c in range(per):
            at = plan_at(nsh, c)
            col = me * per + c
            back = lax.rem(col + span - shift_y[j], span)
            plan_ref[j, at] = (back + shift_y[j] >= span).astype(jnp.int32)
            plan_ref[j, at + 1] = (back // per) ^ me
            plan_ref[j, at + 2] = lax.rem(back, per)
            ahead = lax.rem(col + shift_y[j], span)
            plan_ref[j, at + 3] = (ahead // per) ^ me
            plan_ref[j, at + 4] = lax.rem(ahead, per)
    for copy in copies[3:]:
        copy.wait()
    units = [(c, f, a) for c in range(per) for f in range(fl) for a in range(ri)]
    for t in range(npw // LANES):
        at = slice(t * LANES, (t + 1) * LANES)
        x = jnp.concatenate([vec_ref[a, 0, c, f, :, at] for c, f, a in units], axis=0)
        out_ref[at, :] = x.T
    wide = jnp.concatenate([den_ref[a, 0, c, f].astype(jnp.float32) for c, f, a in units], axis=1)
    out_ref[pl.ds(npw, nb), :] = wide.astype(jnp.bfloat16)


def pack(vectors, density, shells, shift_x, shift_y, kx_count, ky_count):
    ri, _, per, fl, nb, npw = vectors.shape
    transfers, nsh, _ = shells.shape
    if kx_count <= DIRECT:
        branches = 1 + transfers
    else:
        branches = len(stages(kx_count)) * transfers // 2

    def kernel(*refs):
        pack_kernel(*refs, kx_count=kx_count, ky_count=ky_count)

    out = pl.pallas_call(
        kernel,
        in_specs=[HBM] * 5,
        out_specs=[VM, SM] + [SM] * branches,
        out_shape=[
            jax.ShapeDtypeStruct((npw + nb, LANES), jnp.bfloat16),
            jax.ShapeDtypeStruct((transfers, plan_at(nsh, per)), jnp.int32),
        ]
        + [jax.ShapeDtypeStruct((1,), jnp.int32)] * branches,
        scratch_shapes=[
            pltpu.VMEM(vectors.shape, vectors.dtype),
            pltpu.VMEM(density.shape, density.dtype),
            pltpu.SMEM((transfers, 2, nsh), shells.dtype),
            pltpu.SMEM(shift_x.shape, shift_x.dtype),
            pltpu.SMEM(shift_y.shape, shift_y.dtype),
            pltpu.SemaphoreType.DMA((5,)),
        ],
        compiler_params=params(4),
        name="pack_columns",
    )(*[in_hbm(x) for x in (vectors, density, jnp.transpose(shells, (0, 2, 1)), shift_x, shift_y)])
    return out[0], out[1], [x.reshape(()) for x in out[2:]]


def arrivals(own, chosen, transfers, kx_count, ky_count):
    def moved(part, dx):
        pairs = [
            (((x + dx) % kx_count) * ky_count + y, x * ky_count + y) for x in range(kx_count) for y in range(ky_count)
        ]
        return lax.ppermute(part, ("kx", "ky"), pairs)

    if kx_count <= DIRECT:

        def together(members):
            return lambda x, *_: tuple([moved(x, d) for d in members] + [x] * (transfers - len(members)))

        def singly(x, *indices):
            spare = kx_count - transfers
            return tuple(
                lax.switch(index, [partial(moved, dx=1 + i + d) for d in range(spare)], x)
                for i, index in enumerate(indices)
            )

        branches = [together(m) for m in subsets(kx_count)]
        if kx_count - 1 > TOGETHER:
            branches.append(singly)
        return list(lax.switch(chosen[0], branches, own, *chosen[1:]))

    parts = [own] * transfers
    at = 0
    for place, radix in stages(kx_count):

        def pair(a, b):
            return lambda x, y: tuple(moved(p, d * place) if d else p for p, d in ((x, a), (y, b)))

        branches = [pair(a, b) for a in range(radix) for b in range(radix)]
        for j in range(0, transfers, 2):
            parts[j : j + 2] = lax.switch(chosen[at], branches, *parts[j : j + 2])
            at += 1
    return parts


def across_ky(part, count, by):
    return lax.ppermute(part, "ky", [(i, i ^ by) for i in range(count)])


def shifted_tiles(tiles, turn, keep, above, below, zero):
    moved = [pltpu.roll(x, turn, 1) for x in tiles]
    out = []
    for t, x in enumerate(moved):
        other = zero
        if t % PER_PLANE > 0:
            other = jnp.where(above, moved[t - 1], other)
        if t % PER_PLANE < PER_PLANE - 1:
            other = jnp.where(below, moved[t + 1], other)
        out.append(jnp.where(keep, x, other))
    return out


def split(x):
    high = x.astype(jnp.bfloat16)
    return high, (x - high.astype(jnp.float32)).astype(jnp.bfloat16)


def nt(a, b):
    return lax.dot_general(a, b, (((1,), (1,)), ((), ())), preferred_element_type=jnp.float32)


def form_factors(near_ref, far_ref, shift, dims, nsh):
    ri, per, fl, nb, npw = dims
    lane = lax.broadcasted_iota(jnp.int32, (nb, LANES), 1)
    lane_row, lane_col = lane // GB, lane % GB
    unit = lane // (ri * nb)
    long_lane = lax.broadcasted_iota(jnp.int32, (nsh * nb, LANES), 1)
    none = jnp.zeros((nb, LANES), jnp.bfloat16)
    moves = []
    for c in range(per):
        moves.append([])
        for l in range(nsh):
            s1, s2 = shift(c, l)
            inside = (lane_col >= s2) & (lane_col < GB + s2)
            keep = inside & (lane_row >= s1) & (lane_row < PER_TILE + s1)
            turn = (s1 * GB + s2 + LANES) & (LANES - 1)
            moves[c].append((turn, keep, inside & (lane_row < s1), inside & (lane_row >= PER_TILE + s1), none))
    plane = PER_PLANE * LANES
    products = {}
    for a in range(ri):
        for c in range(per):
            for f in range(fl):
                own = []
                for l, move in enumerate(moves[c]):
                    planes = []
                    for at in range(0, npw, plane):
                        tiles = [near_ref[a, c, f, :, i : i + LANES] for i in range(at, at + plane, LANES)]
                        planes += shifted_tiles(tiles, *move)
                    own.append(jnp.concatenate(planes, axis=1))
                products[a, c * fl + f] = jnp.dot(
                    jnp.concatenate(own, axis=0), far_ref[:npw, :], preferred_element_type=jnp.float32
                )
    merged = []
    for a in range(ri):
        x = products[a, 0]
        for u in range(1, per * fl):
            x = jnp.where(long_lane // (ri * nb) == u, products[a, u], x)
        merged.append(x)
    other = jnp.where(
        (long_lane // nb) % ri == 1, -pltpu.roll(merged[1], nb, 1), pltpu.roll(merged[1], LANES - nb, 1)
    )
    return merged[0] + other


def density_mix(far_ref, dims):
    ri, per, fl, nb, npw = dims
    lane = lax.broadcasted_iota(jnp.int32, (nb, LANES), 1)
    unit = lane // (ri * nb)
    den = far_ref[npw : npw + nb, :].astype(jnp.float32)
    turned = jnp.where((lane // nb) % ri == 1, pltpu.roll(den, nb, 1), -pltpu.roll(den, LANES - nb, 1))
    zero = jnp.zeros((nb, LANES), jnp.float32)
    plain, crossed = [], []
    for u in range(per * fl):
        for row_plain, row_crossed in ((den, -turned), (turned, den)):
            plain.append(jnp.where(unit == u, row_plain, zero))
            crossed.append(jnp.where(unit == u, row_crossed, zero))
    mix = jnp.concatenate([jnp.concatenate(plain, axis=0), jnp.concatenate(crossed, axis=0)], axis=1)
    return mix.astype(jnp.bfloat16)


def shell_sums(lams, mixes, weights, dims, nsh):
    ri, per, fl, nb, npw = dims
    unit = lax.broadcasted_iota(jnp.int32, (nb, LANES), 1) // (ri * nb)
    halves = [split(lam) for lam in lams]
    lefts = [
        jnp.dot(
            jnp.concatenate(half, axis=1), jnp.concatenate([mix, mix], axis=0), preferred_element_type=jnp.float32
        )
        for half, mix in zip(halves, mixes)
    ]
    scaled = []
    for left, weight in zip(lefts, weights):
        parts = []
        for l in range(nsh):
            here = slice(l * nb, (l + 1) * nb)
            high, low = split(jnp.concatenate([left[here, :LANES], left[here, LANES:]], axis=0) * weight(l))
            parts += [high, high, low]
        scaled.append(jnp.concatenate(parts, axis=1))
    spread = []
    for half in halves:
        parts = []
        for l in range(nsh):
            here = slice(l * nb, (l + 1) * nb)
            high, low = [
                jnp.concatenate(
                    [jnp.where(unit == u, x[here], jnp.zeros_like(x[here])) for u in range(per * fl)], axis=0
                )
                for x in half
            ]
            parts += [high, low, high]
        spread.append(jnp.concatenate(parts, axis=1))
    return [nt(a, b) for a, b in zip(scaled, spread)]


def terms(plan, weights, blocks, own, arrived, dims, transfers):
    ri, per, fl, nb, npw = dims
    nsh = weights.shape[1]
    count = len(blocks)
    wide = per * fl * nb

    def kernel(plan_ref, weight_ref, *refs):
        ins, others, (out_ref, near, far, lam_ref) = refs[:count], refs[count:-4], refs[-4:]
        for j in range(transfers):
            for i, source in enumerate(others):

                @pl.when(plan_ref[j, 0] == i)
                def _():
                    far[j] = source[...]

            for c in range(per):
                at = plan_at(nsh, c)
                for o in range(count):

                    @pl.when(plan_ref[j, at + 1] == o)
                    def _():
                        for a in range(ri):
                            near[j, a, c] = ins[o][a, 0, plan_ref[j, at + 2]]

        for j in range(transfers):

            def shift(c, l):
                return plan_ref[j, 1 + l], plan_ref[j, 1 + nsh + l] + plan_ref[j, plan_at(nsh, c)]

            lam_ref[j] = form_factors(near.at[j], far.at[j], shift, dims, nsh)
        sums = []
        for first in range(0, transfers, BATCH):
            batch = range(first, min(first + BATCH, transfers))
            sums += shell_sums(
                [lam_ref[j] for j in batch],
                [density_mix(far.at[j], dims) for j in batch],
                [lambda l, j=j: weight_ref[j, l] for j in batch],
                dims,
                nsh,
            )
        per_row = LANES // wide
        for j, total in enumerate(sums):
            top = (j // per_row) * ri * nb
            left = (j % per_row) * wide
            out_ref[top : top + ri * nb, left : left + wide] = total

    return pl.pallas_call(
        kernel,
        in_specs=[SM, SM] + [VM] * (count + 1 + len(arrived)),
        out_specs=VM,
        out_shape=jax.ShapeDtypeStruct((transfers * wide // LANES * ri * nb, LANES), jnp.float32),
        scratch_shapes=[
            pltpu.VMEM((transfers, ri, per, fl, nb, npw), blocks[0].dtype),
            pltpu.VMEM((transfers,) + arrived[0].shape, arrived[0].dtype),
            pltpu.VMEM((transfers, nsh * nb, LANES), jnp.float32),
        ],
        compiler_params=params(16),
        name="exchange_terms",
    )(plan, in_hbm(weights), *blocks, own, *arrived)


def collect(plan, sums, dims, transfers, nsh, scale):
    ri, per, fl, nb, npw = dims
    count = len(sums)
    wide = per * fl * nb
    per_row = LANES // wide

    def kernel(plan_ref, *refs):
        ins, out_ref = refs[:-1], refs[-1]
        unit = lax.broadcasted_iota(jnp.int32, (ri * nb, LANES), 1) // (fl * nb)
        total = jnp.zeros((ri * nb, LANES), jnp.float32)
        for j in range(transfers):
            top = (j // per_row) * ri * nb
            parts = [x[top : top + ri * nb, :] for x in ins]
            for c in range(per):
                at = plan_at(nsh, c)
                off, place = plan_ref[j, at + 3], plan_ref[j, at + 4]
                part = parts[0]
                for o in range(1, count):
                    part = jnp.where(off == o, parts[o], part)
                turn = (c * fl * nb - (j % per_row) * wide - place * fl * nb) & (LANES - 1)
                total = total + jnp.where(unit == c, pltpu.roll(part, turn, 1), 0.0)
        total = total * scale
        for a in range(ri):
            for c in range(per):
                for f in range(fl):
                    u = c * fl + f
                    out_ref[a, 0, c, f] = total[a * nb : (a + 1) * nb, u * nb : (u + 1) * nb]

    return pl.pallas_call(
        kernel,
        in_specs=[SM] + [VM] * count,
        out_specs=VM,
        out_shape=jax.ShapeDtypeStruct((ri, 1, per, fl, nb, nb), jnp.float32),
        compiler_params=params(2),
        name="collect_terms",
    )(plan, *sums)


def body(vectors, density, coulomb, shells, shift_x, shift_y):
    kx_count, ky_count = lax.axis_size("kx"), lax.axis_size("ky")
    ri, _, per, fl, nb, npw = vectors.shape
    dims = (ri, per, fl, nb, npw)
    transfers, nsh = coulomb.shape
    own, plan, chosen = pack(vectors, density, shells, shift_x, shift_y, kx_count, ky_count)
    blocks = [vectors] + [across_ky(vectors, ky_count, by) for by in range(1, ky_count)]
    arrived = arrivals(own, chosen, transfers, kx_count, ky_count)
    part = terms(plan, coulomb, blocks, own, arrived, dims, transfers)
    sums = {by: across_ky(part, ky_count, by) for by in range(ky_count - 1, 0, -1)}
    sums = [part] + [sums[by] for by in range(1, ky_count)]
    return collect(plan, sums, dims, transfers, nsh, -1.0 / (transfers * nsh))


def solution(mesh):
    placed = (P(None, "kx", "ky"), P(None, "kx", "ky"), P(), P(), P(), P())
    return jax.shard_map(
        body, mesh=mesh, in_specs=placed, out_specs=P(None, "kx", "ky"), check_vma=False
    )
```

```python
import itertools
import math
from functools import partial

import jax
import jax.numpy as jnp
from jax import lax
from jax.experimental import pallas as pl
from jax.experimental.pallas import tpu as pltpu
from jax.sharding import PartitionSpec as P

GA = 16
GB = 16
LANES = 128
SPAN = 4
PER_TILE = LANES // GB
PER_PLANE = GA // PER_TILE
DIRECT = 8
BATCH = 4
TOGETHER = 3
MIB = 1 << 20
VM = pl.BlockSpec(memory_space=pltpu.VMEM)
SM = pl.BlockSpec(memory_space=pltpu.SMEM)
HBM = pl.BlockSpec(memory_space=pltpu.HBM)


def in_hbm(x):
    return pltpu.with_memory_space_constraint(x, pltpu.HBM)


def params(mib):
    return pltpu.CompilerParams(vmem_limit_bytes=mib * MIB)


def stages(kx_count):
    out, place = [], 1
    while place < kx_count:
        out.append((place, min(4, kx_count // place)))
        place *= out[-1][1]
    return out


def subsets(count):
    out = []
    for size in range(TOGETHER + 1):
        out += sorted(itertools.combinations(range(1, count), size), key=lambda m: m[::-1])
    return out


def traced_binomial(n, k):
    out = n
    for i in range(1, k):
        out = out * (n - i)
    return lax.div(out, jnp.int32(math.factorial(k)))


WIDTH = 3


def plan_at(nsh, c):
    return 1 + 2 * nsh + WIDTH * c


def pack_kernel(vec_hbm, den_hbm, shells_hbm, x_hbm, y_hbm, out_ref, plan_ref, *rest, kx_count, ky_count):
    branch_refs, (vec_ref, den_ref, shells_ref, shift_x, shift_y, sem) = rest[:-6], rest[-6:]
    given = (x_hbm, y_hbm, shells_hbm, den_hbm, vec_hbm)
    held = (shift_x, shift_y, shells_ref, den_ref, vec_ref)
    copies = [pltpu.make_async_copy(src, dst, sem.at[i]) for i, (src, dst) in enumerate(zip(given, held))]
    for copy in copies:
        copy.start()
    for copy in copies[:3]:
        copy.wait()
    ri, _, per, fl, nb, npw = vec_ref.shape
    transfers, _, nsh = shells_ref.shape
    row, me = lax.axis_index("kx"), lax.axis_index("ky")
    span = per * ky_count
    steps = [shift_x[j] for j in range(transfers)]
    if kx_count <= DIRECT:
        order = [jnp.int32(0)] * kx_count
        found = jnp.int32(0)
        members = [jnp.int32(0)] * transfers
        for d in range(1, kx_count):
            used = steps[0] == d
            for q in steps[1:]:
                used = used | (q == d)
            for i in range(transfers):
                members[i] = jnp.where(used & (found == i), d, members[i])
            found = found + used.astype(jnp.int32)
            order[d] = found
        index = jnp.int32(0)
        for i in range(TOGETHER):
            here = found > i
            index = index + jnp.where(here, math.comb(kx_count - 1, i), 0)
            index = index + jnp.where(here, traced_binomial(members[i] - 1, i + 1), 0)
        branch_refs[0][0] = jnp.where(found > TOGETHER, len(subsets(kx_count)), index)
        for i in range(transfers):
            branch_refs[1 + i][0] = jnp.where(found > TOGETHER, members[i] - 1 - i, 0)
        slots = []
        for q in steps:
            slot = jnp.int32(0)
            for d in range(1, kx_count):
                slot = jnp.where(q == d, order[d], slot)
            slots.append(slot)
    else:
        at = 0
        for place, radix in stages(kx_count):
            for j in range(0, transfers, 2):
                digits = [lax.rem(steps[j + i] // place, radix) for i in range(2)]
                branch_refs[at][0] = digits[0] * radix + digits[1]
                at += 1
        slots = [jnp.int32(j + 1) for j in range(transfers)]
    for j in range(transfers):
        plan_ref[j, 0] = slots[j]
        wrap = (row + steps[j] >= kx_count).astype(jnp.int32)
        for l in range(nsh):
            plan_ref[j, 1 + l] = shells_ref[j, 0, l] + wrap
            plan_ref[j, 1 + nsh + l] = shells_ref[j, 1, l]
        for c in range(per):
            at = plan_at(nsh, c)
            col = me * per + c
            back = lax.rem(col + span - shift_y[j], span)
            plan_ref[j, at] = (back + shift_y[j] >= span).astype(jnp.int32)
            plan_ref[j, at + 1] = (back // per) ^ me
            plan_ref[j, at + 2] = lax.rem(back, per)
    for copy in copies[3:]:
        copy.wait()
    units = [(c, f, a) for c in range(per) for f in range(fl) for a in range(ri)]
    for t in range(npw // LANES):
        at = slice(t * LANES, (t + 1) * LANES)
        x = jnp.concatenate([vec_ref[a, 0, c, f, :, at] for c, f, a in units], axis=0)
        out_ref[at, :] = x.T
    wide = jnp.concatenate([den_ref[a, 0, c, f].astype(jnp.float32) for c, f, a in units], axis=1)
    out_ref[pl.ds(npw, nb), :] = wide.astype(jnp.bfloat16)


def pack(vectors, density, shells, shift_x, shift_y, kx_count, ky_count):
    ri, _, per, fl, nb, npw = vectors.shape
    transfers, nsh, _ = shells.shape
    if kx_count <= DIRECT:
        branches = 1 + transfers
    else:
        branches = len(stages(kx_count)) * transfers // 2

    def kernel(*refs):
        pack_kernel(*refs, kx_count=kx_count, ky_count=ky_count)

    out = pl.pallas_call(
        kernel,
        in_specs=[HBM] * 5,
        out_specs=[VM, SM] + [SM] * branches,
        out_shape=[
            jax.ShapeDtypeStruct((npw + nb, LANES), jnp.bfloat16),
            jax.ShapeDtypeStruct((transfers, plan_at(nsh, per)), jnp.int32),
        ]
        + [jax.ShapeDtypeStruct((1,), jnp.int32)] * branches,
        scratch_shapes=[
            pltpu.VMEM(vectors.shape, vectors.dtype),
            pltpu.VMEM(density.shape, density.dtype),
            pltpu.SMEM((transfers, 2, nsh), shells.dtype),
            pltpu.SMEM(shift_x.shape, shift_x.dtype),
            pltpu.SMEM(shift_y.shape, shift_y.dtype),
            pltpu.SemaphoreType.DMA((5,)),
        ],
        compiler_params=params(4),
        name="pack_columns",
    )(*[in_hbm(x) for x in (vectors, density, jnp.transpose(shells, (0, 2, 1)), shift_x, shift_y)])
    return out[0], out[1], [x.reshape(()) for x in out[2:]]


def arrivals(own, chosen, transfers, kx_count, ky_count):
    def moved(part, dx):
        pairs = [
            (((x + dx) % kx_count) * ky_count + y, x * ky_count + y) for x in range(kx_count) for y in range(ky_count)
        ]
        return lax.ppermute(part, ("kx", "ky"), pairs)

    if kx_count <= DIRECT:

        def together(members):
            return lambda x, *_: tuple([moved(x, d) for d in members] + [x] * (transfers - len(members)))

        def singly(x, *indices):
            spare = kx_count - transfers
            return tuple(
                lax.switch(index, [partial(moved, dx=1 + i + d) for d in range(spare)], x)
                for i, index in enumerate(indices)
            )

        branches = [together(m) for m in subsets(kx_count)]
        if kx_count - 1 > TOGETHER:
            branches.append(singly)
        return list(lax.switch(chosen[0], branches, own, *chosen[1:]))

    parts = [own] * transfers
    at = 0
    for place, radix in stages(kx_count):

        def pair(a, b):
            return lambda x, y: tuple(moved(p, d * place) if d else p for p, d in ((x, a), (y, b)))

        branches = [pair(a, b) for a in range(radix) for b in range(radix)]
        for j in range(0, transfers, 2):
            parts[j : j + 2] = lax.switch(chosen[at], branches, *parts[j : j + 2])
            at += 1
    return parts


def across_ky(part, count, by):
    return lax.ppermute(part, "ky", [(i, i ^ by) for i in range(count)])


def shifted_tiles(tiles, turn, keep, above, below, zero):
    moved = [pltpu.roll(x, turn, 1) for x in tiles]
    out = []
    for t, x in enumerate(moved):
        other = zero
        if t % PER_PLANE > 0:
            other = jnp.where(above, moved[t - 1], other)
        if t % PER_PLANE < PER_PLANE - 1:
            other = jnp.where(below, moved[t + 1], other)
        out.append(jnp.where(keep, x, other))
    return out


def split(x):
    high = x.astype(jnp.bfloat16)
    return high, (x - high.astype(jnp.float32)).astype(jnp.bfloat16)


def nt(a, b):
    return lax.dot_general(a, b, (((1,), (1,)), ((), ())), preferred_element_type=jnp.float32)


def form_factors(near_ref, far_ref, shift, dims, nsh):
    ri, per, fl, nb, npw = dims
    lane = lax.broadcasted_iota(jnp.int32, (nb, LANES), 1)
    lane_row, lane_col = lane // GB, lane % GB
    unit = lane // (ri * nb)
    long_lane = lax.broadcasted_iota(jnp.int32, (nsh * nb, LANES), 1)
    none = jnp.zeros((nb, LANES), jnp.bfloat16)
    moves = []
    for c in range(per):
        moves.append([])
        for l in range(nsh):
            s1, s2 = shift(c, l)
            inside = (lane_col >= s2) & (lane_col < GB + s2)
            keep = inside & (lane_row >= s1) & (lane_row < PER_TILE + s1)
            turn = (s1 * GB + s2 + LANES) & (LANES - 1)
            moves[c].append((turn, keep, inside & (lane_row < s1), inside & (lane_row >= PER_TILE + s1), none))
    plane = PER_PLANE * LANES
    products = {}
    for a in range(ri):
        for c in range(per):
            for f in range(fl):
                own = []
                for l, move in enumerate(moves[c]):
                    planes = []
                    for at in range(0, npw, plane):
                        tiles = [near_ref[a, c, f, :, i : i + LANES] for i in range(at, at + plane, LANES)]
                        planes += shifted_tiles(tiles, *move)
                    own.append(jnp.concatenate(planes, axis=1))
                products[a, c * fl + f] = jnp.dot(
                    jnp.concatenate(own, axis=0), far_ref[:npw, :], preferred_element_type=jnp.float32
                )
    merged = []
    for a in range(ri):
        x = products[a, 0]
        for u in range(1, per * fl):
            x = jnp.where(long_lane // (ri * nb) == u, products[a, u], x)
        merged.append(x)
    other = jnp.where(
        (long_lane // nb) % ri == 1, -pltpu.roll(merged[1], nb, 1), pltpu.roll(merged[1], LANES - nb, 1)
    )
    return merged[0] + other


def density_mix(far_ref, dims):
    ri, per, fl, nb, npw = dims
    lane = lax.broadcasted_iota(jnp.int32, (nb, LANES), 1)
    unit = lane // (ri * nb)
    den = far_ref[npw : npw + nb, :].astype(jnp.float32)
    turned = jnp.where((lane // nb) % ri == 1, pltpu.roll(den, nb, 1), -pltpu.roll(den, LANES - nb, 1))
    zero = jnp.zeros((nb, LANES), jnp.float32)
    plain, crossed = [], []
    for u in range(per * fl):
        for row_plain, row_crossed in ((den, -turned), (turned, den)):
            plain.append(jnp.where(unit == u, row_plain, zero))
            crossed.append(jnp.where(unit == u, row_crossed, zero))
    mix = jnp.concatenate([jnp.concatenate(plain, axis=0), jnp.concatenate(crossed, axis=0)], axis=1)
    return mix.astype(jnp.bfloat16)


def shell_sums(lams, mixes, weights, dims, nsh):
    ri, per, fl, nb, npw = dims
    unit = lax.broadcasted_iota(jnp.int32, (nb, LANES), 1) // (ri * nb)
    halves = [split(lam) for lam in lams]
    lefts = [
        jnp.dot(
            jnp.concatenate(half, axis=1), jnp.concatenate([mix, mix], axis=0), preferred_element_type=jnp.float32
        )
        for half, mix in zip(halves, mixes)
    ]
    scaled = []
    for left, weight in zip(lefts, weights):
        parts = []
        for l in range(nsh):
            here = slice(l * nb, (l + 1) * nb)
            high, low = split(jnp.concatenate([left[here, :LANES], left[here, LANES:]], axis=0) * weight(l))
            parts += [high, high, low]
        scaled.append(jnp.concatenate(parts, axis=1))
    spread = []
    for half in halves:
        parts = []
        for l in range(nsh):
            here = slice(l * nb, (l + 1) * nb)
            high, low = [
                jnp.concatenate(
                    [jnp.where(unit == u, x[here], jnp.zeros_like(x[here])) for u in range(per * fl)], axis=0
                )
                for x in half
            ]
            parts += [high, low, high]
        spread.append(jnp.concatenate(parts, axis=1))
    return [nt(a, b) for a, b in zip(scaled, spread)]


def terms(plan, weights, blocks, own, arrived, dims, transfers):
    ri, per, fl, nb, npw = dims
    nsh = weights.shape[1]
    count = len(blocks)
    wide = per * fl * nb

    def kernel(plan_ref, weight_ref, *refs):
        ins, others, out_refs = refs[:count], refs[count : -3 - count], refs[-3 - count : -3]
        near, far, lam_ref = refs[-3:]
        for j in range(transfers):
            for i, source in enumerate(others):

                @pl.when(plan_ref[j, 0] == i)
                def _():
                    far[j] = source[...]

            for c in range(per):
                at = plan_at(nsh, c)
                for o in range(count):

                    @pl.when(plan_ref[j, at + 1] == o)
                    def _():
                        for a in range(ri):
                            near[j, a, c] = ins[o][a, 0, plan_ref[j, at + 2]]

        for j in range(transfers):

            def shift(c, l):
                return plan_ref[j, 1 + l], plan_ref[j, 1 + nsh + l] + plan_ref[j, plan_at(nsh, c)]

            lam_ref[j] = form_factors(near.at[j], far.at[j], shift, dims, nsh)
        sums = []
        for first in range(0, transfers, BATCH):
            batch = range(first, min(first + BATCH, transfers))
            sums += shell_sums(
                [lam_ref[j] for j in batch],
                [density_mix(far.at[j], dims) for j in batch],
                [lambda l, j=j: weight_ref[j, l] for j in batch],
                dims,
                nsh,
            )
        column = lax.broadcasted_iota(jnp.int32, (ri * nb, LANES), 1) // (fl * nb)
        parcels = [jnp.zeros((ri * nb, LANES), jnp.float32)] * count
        for j, total in enumerate(sums):
            filled = jnp.concatenate([total] * (LANES // wide), axis=1)
            for c in range(per):
                at = plan_at(nsh, c)
                owner, place = plan_ref[j, at + 1], plan_ref[j, at + 2]
                turned = pltpu.roll(filled, ((place - c) * (fl * nb)) & (LANES - 1), 1)
                for o in range(count):
                    chosen = jnp.where(owner == o, place, -1)
                    parcels[o] = parcels[o] + jnp.where(column == chosen, turned, 0.0)
        for out_ref, parcel in zip(out_refs, parcels):
            out_ref[...] = parcel[:, :wide]

    return pl.pallas_call(
        kernel,
        in_specs=[SM, SM] + [VM] * (count + 1 + len(arrived)),
        out_specs=[VM] * count,
        out_shape=[jax.ShapeDtypeStruct((ri * nb, wide), jnp.float32)] * count,
        scratch_shapes=[
            pltpu.VMEM((transfers, ri, per, fl, nb, npw), blocks[0].dtype),
            pltpu.VMEM((transfers,) + arrived[0].shape, arrived[0].dtype),
            pltpu.VMEM((transfers, nsh * nb, LANES), jnp.float32),
        ],
        compiler_params=params(16),
        name="exchange_terms",
    )(plan, in_hbm(weights), *blocks, own, *arrived)


def collect(parcels, dims, scale):
    ri, per, fl, nb, npw = dims

    def kernel(*refs):
        ins, out_ref = refs[:-1], refs[-1]
        total = ins[0][...]
        for x in ins[1:]:
            total = total + x[...]
        total = total * scale
        for a in range(ri):
            for c in range(per):
                for f in range(fl):
                    u = c * fl + f
                    out_ref[a, 0, c, f] = total[a * nb : (a + 1) * nb, u * nb : (u + 1) * nb]

    return pl.pallas_call(
        kernel,
        in_specs=[VM] * len(parcels),
        out_specs=VM,
        out_shape=jax.ShapeDtypeStruct((ri, 1, per, fl, nb, nb), jnp.float32),
        compiler_params=params(2),
        name="collect_terms",
    )(*parcels)


def body(vectors, density, coulomb, shells, shift_x, shift_y):
    kx_count, ky_count = lax.axis_size("kx"), lax.axis_size("ky")
    ri, _, per, fl, nb, npw = vectors.shape
    dims = (ri, per, fl, nb, npw)
    transfers, nsh = coulomb.shape
    own, plan, chosen = pack(vectors, density, shells, shift_x, shift_y, kx_count, ky_count)
    blocks = [vectors] + [across_ky(vectors, ky_count, by) for by in range(1, ky_count)]
    arrived = arrivals(own, chosen, transfers, kx_count, ky_count)
    parcels = terms(plan, coulomb, blocks, own, arrived, dims, transfers)
    sent = {by: across_ky(parcels[by], ky_count, by) for by in range(ky_count - 1, 0, -1)}
    received = [parcels[0]] + [sent[by] for by in range(1, ky_count)]
    return collect(received, dims, -1.0 / (transfers * nsh))


def solution(mesh):
    placed = (P(None, "kx", "ky"), P(None, "kx", "ky"), P(), P(), P(), P())
    return jax.shard_map(
        body, mesh=mesh, in_specs=placed, out_specs=P(None, "kx", "ky"), check_vma=False
    )
```

```python
import itertools
import math
from functools import partial

import jax
import jax.numpy as jnp
from jax import lax
from jax.experimental import pallas as pl
from jax.experimental.pallas import tpu as pltpu
from jax.sharding import PartitionSpec as P

GA = 16
GB = 16
LANES = 128
SPAN = 4
PER_TILE = LANES // GB
PER_PLANE = GA // PER_TILE
DIRECT = 8
BATCH = 4
TOGETHER = 3
MIB = 1 << 20
VM = pl.BlockSpec(memory_space=pltpu.VMEM)
SM = pl.BlockSpec(memory_space=pltpu.SMEM)
HBM = pl.BlockSpec(memory_space=pltpu.HBM)


def in_hbm(x):
    return pltpu.with_memory_space_constraint(x, pltpu.HBM)


def params(mib):
    return pltpu.CompilerParams(vmem_limit_bytes=mib * MIB)


def stages(kx_count):
    out, place = [], 1
    while place < kx_count:
        out.append((place, min(4, kx_count // place)))
        place *= out[-1][1]
    return out


def subsets(count):
    out = []
    for size in range(TOGETHER + 1):
        out += sorted(itertools.combinations(range(1, count), size), key=lambda m: m[::-1])
    return out


def traced_binomial(n, k):
    out = n
    for i in range(1, k):
        out = out * (n - i)
    return lax.div(out, jnp.int32(math.factorial(k)))


WIDTH = 3


def plan_at(nsh, c):
    return 1 + 2 * nsh + WIDTH * c


def pack_kernel(vec_hbm, den_hbm, shells_hbm, x_hbm, y_hbm, out_ref, plan_ref, *rest, kx_count, ky_count):
    branch_refs, (vec_ref, den_ref, shells_ref, shift_x, shift_y, sem) = rest[:-6], rest[-6:]
    given = (x_hbm, y_hbm, shells_hbm, den_hbm, vec_hbm)
    held = (shift_x, shift_y, shells_ref, den_ref, vec_ref)
    copies = [pltpu.make_async_copy(src, dst, sem.at[i]) for i, (src, dst) in enumerate(zip(given, held))]
    for copy in copies:
        copy.start()
    for copy in copies[:3]:
        copy.wait()
    ri, _, per, fl, nb, npw = vec_ref.shape
    transfers, _, nsh = shells_ref.shape
    row, me = lax.axis_index("kx"), lax.axis_index("ky")
    span = per * ky_count
    steps = [shift_x[j] for j in range(transfers)]
    if kx_count <= DIRECT:
        order = [jnp.int32(0)] * kx_count
        found = jnp.int32(0)
        members = [jnp.int32(0)] * transfers
        for d in range(1, kx_count):
            used = steps[0] == d
            for q in steps[1:]:
                used = used | (q == d)
            for i in range(transfers):
                members[i] = jnp.where(used & (found == i), d, members[i])
            found = found + used.astype(jnp.int32)
            order[d] = found
        index = jnp.int32(0)
        for i in range(TOGETHER):
            here = found > i
            index = index + jnp.where(here, math.comb(kx_count - 1, i), 0)
            index = index + jnp.where(here, traced_binomial(members[i] - 1, i + 1), 0)
        branch_refs[0][0] = jnp.where(found > TOGETHER, len(subsets(kx_count)), index)
        for i in range(transfers):
            branch_refs[1 + i][0] = jnp.where(found > TOGETHER, members[i] - 1 - i, 0)
        slots = []
        for q in steps:
            slot = jnp.int32(0)
            for d in range(1, kx_count):
                slot = jnp.where(q == d, order[d], slot)
            slots.append(slot)
    else:
        at = 0
        for place, radix in stages(kx_count):
            for j in range(0, transfers, 2):
                digits = [lax.rem(steps[j + i] // place, radix) for i in range(2)]
                branch_refs[at][0] = digits[0] * radix + digits[1]
                at += 1
        slots = [jnp.int32(j + 1) for j in range(transfers)]
    for j in range(transfers):
        plan_ref[j, 0] = slots[j]
        wrap = (row + steps[j] >= kx_count).astype(jnp.int32)
        for l in range(nsh):
            plan_ref[j, 1 + l] = shells_ref[j, 0, l] + wrap
            plan_ref[j, 1 + nsh + l] = shells_ref[j, 1, l]
        for c in range(per):
            at = plan_at(nsh, c)
            col = me * per + c
            back = lax.rem(col + span - shift_y[j], span)
            plan_ref[j, at] = (back + shift_y[j] >= span).astype(jnp.int32)
            plan_ref[j, at + 1] = (back // per) ^ me
            plan_ref[j, at + 2] = lax.rem(back, per)
    for copy in copies[3:]:
        copy.wait()
    units = [(c, f, a) for c in range(per) for f in range(fl) for a in range(ri)]
    for t in range(npw // LANES):
        at = slice(t * LANES, (t + 1) * LANES)
        x = jnp.concatenate([vec_ref[a, 0, c, f, :, at] for c, f, a in units], axis=0)
        out_ref[at, :] = x.T
    wide = jnp.concatenate([den_ref[a, 0, c, f].astype(jnp.float32) for c, f, a in units], axis=1)
    out_ref[pl.ds(npw, nb), :] = wide.astype(jnp.bfloat16)


def pack(vectors, density, shells, shift_x, shift_y, kx_count, ky_count):
    ri, _, per, fl, nb, npw = vectors.shape
    transfers, nsh, _ = shells.shape
    if kx_count <= DIRECT:
        branches = 1 + transfers
    else:
        branches = len(stages(kx_count)) * transfers // 2

    def kernel(*refs):
        pack_kernel(*refs, kx_count=kx_count, ky_count=ky_count)

    out = pl.pallas_call(
        kernel,
        in_specs=[HBM] * 5,
        out_specs=[VM, SM] + [SM] * branches,
        out_shape=[
            jax.ShapeDtypeStruct((npw + nb, LANES), jnp.bfloat16),
            jax.ShapeDtypeStruct((transfers, plan_at(nsh, per)), jnp.int32),
        ]
        + [jax.ShapeDtypeStruct((1,), jnp.int32)] * branches,
        scratch_shapes=[
            pltpu.VMEM(vectors.shape, vectors.dtype),
            pltpu.VMEM(density.shape, density.dtype),
            pltpu.SMEM((transfers, 2, nsh), shells.dtype),
            pltpu.SMEM(shift_x.shape, shift_x.dtype),
            pltpu.SMEM(shift_y.shape, shift_y.dtype),
            pltpu.SemaphoreType.DMA((5,)),
        ],
        compiler_params=params(4),
        name="pack_columns",
    )(*[in_hbm(x) for x in (vectors, density, jnp.transpose(shells, (0, 2, 1)), shift_x, shift_y)])
    return out[0], out[1], [x.reshape(()) for x in out[2:]]


def arrivals(own, chosen, transfers, kx_count, ky_count):
    def moved(part, dx):
        pairs = [
            (((x + dx) % kx_count) * ky_count + y, x * ky_count + y) for x in range(kx_count) for y in range(ky_count)
        ]
        return lax.ppermute(part, ("kx", "ky"), pairs)

    if kx_count <= DIRECT:

        def together(members):
            return lambda x, *_: tuple([moved(x, d) for d in members] + [x] * (transfers - len(members)))

        def singly(x, *indices):
            spare = kx_count - transfers
            return tuple(
                lax.switch(index, [partial(moved, dx=1 + i + d) for d in range(spare)], x)
                for i, index in enumerate(indices)
            )

        branches = [together(m) for m in subsets(kx_count)]
        if kx_count - 1 > TOGETHER:
            branches.append(singly)
        return list(lax.switch(chosen[0], branches, own, *chosen[1:]))

    parts = [own] * transfers
    at = 0
    for place, radix in stages(kx_count):

        def pair(a, b):
            return lambda x, y: tuple(moved(p, d * place) if d else p for p, d in ((x, a), (y, b)))

        branches = [pair(a, b) for a in range(radix) for b in range(radix)]
        for j in range(0, transfers, 2):
            parts[j : j + 2] = lax.switch(chosen[at], branches, *parts[j : j + 2])
            at += 1
    return parts


def across_ky(part, count, by):
    return lax.ppermute(part, "ky", [(i, i ^ by) for i in range(count)])


def shifted_tiles(tiles, turn, keep, above, below, zero):
    moved = [pltpu.roll(x, turn, 1) for x in tiles]
    out = []
    for t, x in enumerate(moved):
        other = zero
        if t % PER_PLANE > 0:
            other = jnp.where(above, moved[t - 1], other)
        if t % PER_PLANE < PER_PLANE - 1:
            other = jnp.where(below, moved[t + 1], other)
        out.append(jnp.where(keep, x, other))
    return out


def split(x):
    high = x.astype(jnp.bfloat16)
    return high, (x - high.astype(jnp.float32)).astype(jnp.bfloat16)


def nt(a, b):
    return lax.dot_general(a, b, (((1,), (1,)), ((), ())), preferred_element_type=jnp.float32)


def form_factors(near, far_ref, shift, dims, nsh):
    ri, per, fl, nb, npw = dims
    lane = lax.broadcasted_iota(jnp.int32, (nb, LANES), 1)
    lane_row, lane_col = lane // GB, lane % GB
    unit = lane // (ri * nb)
    long_lane = lax.broadcasted_iota(jnp.int32, (nsh * nb, LANES), 1)
    none = jnp.zeros((nb, LANES), jnp.bfloat16)
    moves = []
    for c in range(per):
        moves.append([])
        for l in range(nsh):
            s1, s2 = shift(c, l)
            inside = (lane_col >= s2) & (lane_col < GB + s2)
            keep = inside & (lane_row >= s1) & (lane_row < PER_TILE + s1)
            turn = (s1 * GB + s2 + LANES) & (LANES - 1)
            moves[c].append((turn, keep, inside & (lane_row < s1), inside & (lane_row >= PER_TILE + s1), none))
    plane = PER_PLANE * LANES
    products = {}
    for a in range(ri):
        for c in range(per):
            for f in range(fl):
                own = []
                for l, move in enumerate(moves[c]):
                    planes = []
                    for at in range(0, npw, plane):
                        tiles = [near(a, c, f, i) for i in range(at, at + plane, LANES)]
                        planes += shifted_tiles(tiles, *move)
                    own.append(jnp.concatenate(planes, axis=1))
                products[a, c * fl + f] = jnp.dot(
                    jnp.concatenate(own, axis=0), far_ref[:npw, :], preferred_element_type=jnp.float32
                )
    merged = []
    for a in range(ri):
        x = products[a, 0]
        for u in range(1, per * fl):
            x = jnp.where(long_lane // (ri * nb) == u, products[a, u], x)
        merged.append(x)
    other = jnp.where(
        (long_lane // nb) % ri == 1, -pltpu.roll(merged[1], nb, 1), pltpu.roll(merged[1], LANES - nb, 1)
    )
    return merged[0] + other


def density_mix(far_ref, dims):
    ri, per, fl, nb, npw = dims
    lane = lax.broadcasted_iota(jnp.int32, (nb, LANES), 1)
    unit = lane // (ri * nb)
    den = far_ref[npw : npw + nb, :].astype(jnp.float32)
    turned = jnp.where((lane // nb) % ri == 1, pltpu.roll(den, nb, 1), -pltpu.roll(den, LANES - nb, 1))
    zero = jnp.zeros((nb, LANES), jnp.float32)
    plain, crossed = [], []
    for u in range(per * fl):
        for row_plain, row_crossed in ((den, -turned), (turned, den)):
            plain.append(jnp.where(unit == u, row_plain, zero))
            crossed.append(jnp.where(unit == u, row_crossed, zero))
    mix = jnp.concatenate([jnp.concatenate(plain, axis=0), jnp.concatenate(crossed, axis=0)], axis=1)
    return mix.astype(jnp.bfloat16)


def shell_sums(lams, mixes, weights, dims, nsh):
    ri, per, fl, nb, npw = dims
    unit = lax.broadcasted_iota(jnp.int32, (nb, LANES), 1) // (ri * nb)
    halves = [split(lam) for lam in lams]
    lefts = [
        jnp.dot(
            jnp.concatenate(half, axis=1), jnp.concatenate([mix, mix], axis=0), preferred_element_type=jnp.float32
        )
        for half, mix in zip(halves, mixes)
    ]
    scaled = []
    for left, weight in zip(lefts, weights):
        parts = []
        for l in range(nsh):
            here = slice(l * nb, (l + 1) * nb)
            high, low = split(jnp.concatenate([left[here, :LANES], left[here, LANES:]], axis=0) * weight(l))
            parts += [high, high, low]
        scaled.append(jnp.concatenate(parts, axis=1))
    spread = []
    for half in halves:
        parts = []
        for l in range(nsh):
            here = slice(l * nb, (l + 1) * nb)
            high, low = [
                jnp.concatenate(
                    [jnp.where(unit == u, x[here], jnp.zeros_like(x[here])) for u in range(per * fl)], axis=0
                )
                for x in half
            ]
            parts += [high, low, high]
        spread.append(jnp.concatenate(parts, axis=1))
    return [nt(a, b) for a, b in zip(scaled, spread)]


def terms(plan, weights, blocks, own, arrived, dims, transfers):
    ri, per, fl, nb, npw = dims
    nsh = weights.shape[1]
    count = len(blocks)
    wide = per * fl * nb

    def kernel(plan_ref, weight_ref, *refs):
        ins, others, out_refs = refs[:count], refs[count : -2 - count], refs[-2 - count : -2]
        far, lam_ref = refs[-2:]
        for j in range(transfers):
            for i, source in enumerate(others):

                @pl.when(plan_ref[j, 0] == i)
                def _():
                    far[j] = source[...]

        for j in range(transfers):

            def shift(c, l):
                return plan_ref[j, 1 + l], plan_ref[j, 1 + nsh + l] + plan_ref[j, plan_at(nsh, c)]

            def near(a, c, f, i):
                owner, place = plan_ref[j, plan_at(nsh, c) + 1], plan_ref[j, plan_at(nsh, c) + 2]
                out = ins[0][a, 0, place, f, :, i : i + LANES]
                for o in range(1, count):
                    out = jnp.where(owner == o, ins[o][a, 0, place, f, :, i : i + LANES], out)
                return out

            lam_ref[j] = form_factors(near, far.at[j], shift, dims, nsh)
        sums = []
        for first in range(0, transfers, BATCH):
            batch = range(first, min(first + BATCH, transfers))
            sums += shell_sums(
                [lam_ref[j] for j in batch],
                [density_mix(far.at[j], dims) for j in batch],
                [lambda l, j=j: weight_ref[j, l] for j in batch],
                dims,
                nsh,
            )
        column = lax.broadcasted_iota(jnp.int32, (ri * nb, LANES), 1) // (fl * nb)
        parcels = [jnp.zeros((ri * nb, LANES), jnp.float32)] * count
        for j, total in enumerate(sums):
            filled = jnp.concatenate([total] * (LANES // wide), axis=1)
            for c in range(per):
                at = plan_at(nsh, c)
                owner, place = plan_ref[j, at + 1], plan_ref[j, at + 2]
                turned = pltpu.roll(filled, ((place - c) * (fl * nb)) & (LANES - 1), 1)
                for o in range(count):
                    chosen = jnp.where(owner == o, place, -1)
                    parcels[o] = parcels[o] + jnp.where(column == chosen, turned, 0.0)
        for out_ref, parcel in zip(out_refs, parcels):
            out_ref[...] = parcel[:, :wide]

    return pl.pallas_call(
        kernel,
        in_specs=[SM, SM] + [VM] * (count + 1 + len(arrived)),
        out_specs=[VM] * count,
        out_shape=[jax.ShapeDtypeStruct((ri * nb, wide), jnp.float32)] * count,
        scratch_shapes=[
            pltpu.VMEM((transfers,) + arrived[0].shape, arrived[0].dtype),
            pltpu.VMEM((transfers, nsh * nb, LANES), jnp.float32),
        ],
        compiler_params=params(16),
        name="exchange_terms",
    )(plan, in_hbm(weights), *blocks, own, *arrived)


def collect(parcels, dims, scale):
    ri, per, fl, nb, npw = dims

    def kernel(*refs):
        ins, out_ref = refs[:-1], refs[-1]
        total = ins[0][...]
        for x in ins[1:]:
            total = total + x[...]
        total = total * scale
        for a in range(ri):
            for c in range(per):
                for f in range(fl):
                    u = c * fl + f
                    out_ref[a, 0, c, f] = total[a * nb : (a + 1) * nb, u * nb : (u + 1) * nb]

    return pl.pallas_call(
        kernel,
        in_specs=[VM] * len(parcels),
        out_specs=VM,
        out_shape=jax.ShapeDtypeStruct((ri, 1, per, fl, nb, nb), jnp.float32),
        compiler_params=params(2),
        name="collect_terms",
    )(*parcels)


def body(vectors, density, coulomb, shells, shift_x, shift_y):
    kx_count, ky_count = lax.axis_size("kx"), lax.axis_size("ky")
    ri, _, per, fl, nb, npw = vectors.shape
    dims = (ri, per, fl, nb, npw)
    transfers, nsh = coulomb.shape
    own, plan, chosen = pack(vectors, density, shells, shift_x, shift_y, kx_count, ky_count)
    blocks = [vectors] + [across_ky(vectors, ky_count, by) for by in range(1, ky_count)]
    arrived = arrivals(own, chosen, transfers, kx_count, ky_count)
    parcels = terms(plan, coulomb, blocks, own, arrived, dims, transfers)
    sent = {by: across_ky(parcels[by], ky_count, by) for by in range(ky_count - 1, 0, -1)}
    received = [parcels[0]] + [sent[by] for by in range(1, ky_count)]
    return collect(received, dims, -1.0 / (transfers * nsh))


def solution(mesh):
    placed = (P(None, "kx", "ky"), P(None, "kx", "ky"), P(), P(), P(), P())
    return jax.shard_map(
        body, mesh=mesh, in_specs=placed, out_specs=P(None, "kx", "ky"), check_vma=False
    )
```
